32 devices in a mesh: grp: 2 (over x), ha: 8 (over z, y), col: 2 (over core).
Axes of the slice: x: 2, y: 2, z: 4, core: 2. Of those that a mesh axis runs over, the one named last changes fastest.
Arguments:
- latent: bfloat16 [2, 64, 128, 384], P('grp', 'ha', None, 'col'), parts along dimension 0, may hold values from -6 to 6
- up_weight: bfloat16 [4, 4, 384, 192], replicated, may hold values from -0.15625 to 0.15625
- conv_one: bfloat16 [3, 3, 192, 192], replicated, may hold values from -0.15625 to 0.15625
- gain_one: float32 [192], replicated, may hold values from 0.1 to 1.9
- conv_two: bfloat16 [3, 3, 192, 192], replicated, may hold values from -0.15625 to 0.15625
- gain_two: float32 [192], replicated, may hold values from 0.1 to 1.9
Outputs:
- decoded: bfloat16 [2, 128, 256, 192], P('grp', 'ha', 'col'), parts along dimension 0
The draws below stay inside these ranges and needn't reach their ends.
There are 2 independent parts, one for each index of `grp`. The reference program is written for one: setup_inputs(seed, part) draws one part's arguments, and reference() takes and returns one part's arrays. A program takes and returns all parts, laid end to end along the dimension named above; an argument that names none is the same for every part. Nothing has to cross between parts.
All inputs are finite; a program needn't handle non-finite values.
Results may differ from the reference program's by a relative error of at most 0.008.
Values may be sent and summed in bfloat16 or wider, within the bound.
A program may use at most 64 MiB of HBM per device.

```python
import jax
import jax.numpy as jnp
from jax import lax

CI = 384
C = 192
F = 1
W = 128
H = 64


def shard_levels(rng, shape, cuts, low, high):
    level, own = 1.0, jax.random.fold_in(rng, 6)
    for position, parts in cuts:
        heights = jnp.exp(jax.random.uniform(jax.random.fold_in(own, position), (parts,), jnp.float32, low / len(cuts), high / len(cuts)))
        level = level * jnp.repeat(heights, shape[position] // parts).reshape([-1 if axis == position else 1 for axis in range(len(shape))])
    return level


def noise(rng, extent, scale, most, pieces=(), kind=jnp.bfloat16):
    result = scale * jax.random.normal(rng, extent, jnp.float32)
    if pieces:
        result = result * shard_levels(rng, extent, pieces, -0.22, 0.18)
    return jnp.clip(result, -most, most).astype(kind)


def setup_inputs(seed: int = 0, part: int = 0) -> dict:
    keys = jax.random.split(jax.random.key(seed), 7)
    part_splits = jax.random.split(jax.random.fold_in(keys[6], part), 7)
    return {
        "latent": noise(part_splits[0], (F, H, W, CI), 1.0, 6.0, ((1, 8), (3, 2))),
        "up_weight": noise(keys[1], (4, 4, CI, C), (4 * CI) ** -0.5, 0.15625),
        "conv_one": noise(keys[2], (3, 3, C, C), (9 * C) ** -0.5, 0.15625),
        "gain_one": jnp.clip(1.0 + 0.18 * jax.random.normal(keys[3], (C,), jnp.float32), 0.1, 1.9),
        "conv_two": noise(keys[4], (3, 3, C, C), (9 * C) ** -0.5, 0.15625),
        "gain_two": jnp.clip(1.0 + 0.18 * jax.random.normal(keys[5], (C,), jnp.float32), 0.1, 1.9),
    }


phase_taps = (((0, 1), (-1, 3)), ((0, 2), (1, 0)))

def upsample_exact(padded, kernel):
    row_count = padded.shape[1] - 2
    col_count = padded.shape[2] - 2
    wide_input = padded.astype(jnp.float32)
    wide_kernel = kernel.astype(jnp.float32)
    phase_rows = []
    for row_phase in range(2):
        phase_cols = []
        for col_phase in range(2):
            summed = None
            for row_shift, row_tap in phase_taps[row_phase]:
                for col_shift, col_tap in phase_taps[col_phase]:
                    window = wide_input[:, 1 + row_shift:1 + row_shift + row_count, 1 + col_shift:1 + col_shift + col_count, :]
                    product = jnp.einsum('fhwc,cd->fhwd', window, wide_kernel[row_tap, col_tap])
                    summed = product if summed is None else summed + product
            phase_cols.append(summed)
        phase_rows.append(jnp.stack(phase_cols, axis=3))
    joined = jnp.stack(phase_rows, axis=2)
    return joined.reshape(joined.shape[0], 2 * row_count, 2 * col_count, joined.shape[-1])

def activate(field, gain):
    wide = field.astype(jnp.float32)
    stats = lax.optimization_barrier(jnp.mean(wide * wide, axis=-1, keepdims=True))
    normed = wide * lax.rsqrt(stats + 1e-06) * gain
    return jax.nn.silu(normed).astype(jnp.bfloat16)

def convolve(field, weight):
    padded = jnp.pad(field, ((0, 0), (1, 1), (1, 1), (0, 0)))
    return lax.conv_general_dilated(padded.astype(jnp.float32), weight.astype(jnp.float32), (1, 1), 'VALID', dimension_numbers=('NHWC', 'HWIO', 'NHWC'))

def reference(latent, up_weight, conv_one, gain_one, conv_two, gain_two):
    padded = jnp.pad(latent, ((0, 0), (1, 1), (1, 1), (0, 0)))
    upsampled = upsample_exact(padded, up_weight).astype(jnp.bfloat16)
    first_act = activate(upsampled, gain_one)
    hidden = convolve(first_act, conv_one).astype(jnp.bfloat16)
    second_act = activate(hidden, gain_two)
    return (upsampled.astype(jnp.float32) + convolve(second_act, conv_two)).astype(jnp.bfloat16)
```

```python
import functools

import jax
import jax.numpy as jnp
from jax import lax
from jax.experimental import pallas as pl
from jax.experimental.pallas import tpu as pltpu
from jax.sharding import PartitionSpec as P

f32 = jnp.float32
bf16 = jnp.bfloat16
MESH = pl.DeviceIdType.MESH
phase_taps = (((0, 1), (-1, 3)), ((0, 2), (1, 0)))


def activate(wide, half_gain):
    stats = jnp.sum(wide * wide, axis=0, keepdims=True) * (1.0 / wide.shape[0])
    half = wide * lax.rsqrt(stats + 1e-06) * half_gain
    return half * jnp.tanh(half) + half


def block_kernel(
    ha_count, lat, gain_one, gain_two, up_hbm, one_hbm, two_hbm, out,
    up_w, raw, one_w, two_w, field, pairs, ups, first, second, gains, perm,
    edges, halos, obuf, sem, send, recv, done
):
    ha = lax.axis_index("ha")
    col = lax.axis_index("col")
    rows, share, width = lat.shape[1], lat.shape[2], lat.shape[3]
    chans = out.shape[2]
    half = width // 2
    depth = 2 * share
    mine = pl.ds(pl.multiple_of(col * share, share), share)
    other = {"col": 1 - col}
    has_above, has_below = ha > 0, ha < ha_count - 1

    barrier = pltpu.get_barrier_semaphore()
    pl.semaphore_signal(barrier, 1, device_id=other, device_id_type=MESH)

    @pl.when(has_above)
    def _():
        pl.semaphore_signal(barrier, 1, device_id={"ha": ha - 1}, device_id_type=MESH)

    @pl.when(has_below)
    def _():
        pl.semaphore_signal(barrier, 1, device_id={"ha": ha + 1}, device_id_type=MESH)

    own = pltpu.make_async_copy(lat.at[0], field.at[pl.ds(2, rows), mine], sem.at[0])
    own.start()
    raw_copies = [
        pltpu.make_async_copy(src, raw.at[n], sem.at[1 + n])
        for n, src in enumerate((one_hbm, two_hbm))
    ]
    for item in raw_copies:
        item.start()
    up_copies = []
    for rp in range(2):
        for cp in range(2):
            tap = 0
            for _, ra in phase_taps[rp]:
                for _, cb in phase_taps[cp]:
                    up_copies.append(pltpu.make_async_copy(
                        up_hbm.at[ra, cb],
                        up_w.at[rp, cp, :, pl.ds(tap * depth, depth)],
                        sem.at[3],
                    ))
                    tap += 1
    for item in up_copies:
        item.start()

    peers = 1 + jnp.minimum(ha, 1) + jnp.minimum(ha_count - 1 - ha, 1)
    pl.semaphore_wait(barrier, peers)

    def remote(src, dst, target, n):
        return pltpu.make_async_remote_copy(
            src_ref=src, dst_ref=dst, send_sem=send.at[n], recv_sem=recv.at[n],
            device_id=target, device_id_type=MESH,
        )

    top, bottom = field.at[pl.ds(0, 2), mine], field.at[pl.ds(rows + 2, 2), mine]
    side = remote(lat.at[0], field.at[pl.ds(2, rows), mine], other, 0)
    down = remote(lat.at[0, pl.ds(rows - 2, 2)], top, {"ha": ha + 1}, 1)
    up = remote(lat.at[0, pl.ds(0, 2)], bottom, {"ha": ha - 1}, 2)
    pass_top = remote(top, top, other, 3)
    pass_bottom = remote(bottom, bottom, other, 4)
    swaps = [remote(edges.at[n], halos.at[n], other, 5 + n) for n in range(4)]

    @pl.when(has_below)
    def _():
        down.start()

    @pl.when(has_above)
    def _():
        up.start()

    side.start()

    @pl.when(ha == 0)
    def _():
        field[pl.ds(0, 2)] = jnp.zeros((2, depth, width), bf16)

    @pl.when(ha == ha_count - 1)
    def _():
        field[pl.ds(rows + 2, 2)] = jnp.zeros((2, depth, width), bf16)

    for n, gain in enumerate((gain_one, gain_two)):
        gains[n] = jnp.broadcast_to(gain[...] * 0.5, (width, chans)).T
    at = lax.broadcasted_iota(jnp.int32, (2 * width, 2 * width), 0)
    to = lax.broadcasted_iota(jnp.int32, (2 * width, 2 * width), 1)
    source = (to % 2) * width + (to // width) * half + (to % width) // 2
    perm[...] = (source == at).astype(f32).astype(bf16)
    at = lax.broadcasted_iota(jnp.int32, (chans, chans), 0)
    to = lax.broadcasted_iota(jnp.int32, (chans, chans), 1)
    eye = (at == to).astype(f32).astype(bf16)

    for n, turned in enumerate((one_w, two_w)):
        raw_copies[n].wait()
        for a in range(3):
            turned[:, pl.ds(a * 3 * chans, 3 * chans)] = lax.dot_general(
                eye, raw[n, a].reshape(3 * chans, chans), (((1,), (1,)), ((), ())),
                preferred_element_type=f32,
            ).astype(bf16)

    lane = lax.broadcasted_iota(jnp.int32, (depth, width), 1)
    keep = (lane < half) == (col == 0)
    low = lane % half == 0
    high = lane % half == half - 1
    low_col = low & (col == 0)
    high_col = high & (col > 0)
    zero = jnp.zeros((depth, width), bf16)

    def make_pair(n, f, apart):
        near = field[f + apart * col]
        far = pltpu.roll(field[f + apart * (1 - col)], half, 1)
        here = jnp.where(keep, near, far)
        there = jnp.where(keep, far, near)
        pairs[n, 1] = here
        pairs[n, 0] = pltpu.roll(jnp.where(high_col, there, jnp.where(high, zero, here)), 1, 1)
        pairs[n, 2] = pltpu.roll(
            jnp.where(low_col, there, jnp.where(low, zero, here)), width - 1, 1
        )

    cell = lax.broadcasted_iota(jnp.int32, (chans, width), 1)
    blank = jnp.zeros((chans, width), bf16)

    def place(field3, r, value, n):
        field3[r, pl.ds(chans, chans)] = value
        field3[r, pl.ds(0, chans)] = jnp.where(cell == 0, blank, pltpu.roll(value, 1, 1))
        field3[r, pl.ds(2 * chans, chans)] = jnp.where(
            cell == width - 1, blank, pltpu.roll(value, width - 1, 1)
        )
        edges[n] = jnp.where(cell == r + 1, pltpu.roll(value, r + 2 - col, 1), edges[n])

    side_at = pl.ds(pl.multiple_of((1 - col) * 2 * chans, chans), chans)
    side_cell = cell == (1 - col) * (width - 1)

    def join(field3, r, n):
        moved = pltpu.roll(halos[n], width - 2 - r + col, 1)
        field3[r, side_at] = jnp.where(side_cell, moved, field3[r, side_at])

    def upsample(base, count, start, apart, n):
        for rp in range(2):
            parts = []
            for cp in range(2):
                pieces = []
                for dr, _ in phase_taps[rp]:
                    for dc, _ in phase_taps[cp]:
                        pieces.append(jnp.concatenate(
                            [pairs[base + k + 1 + dr, 1 + dc] for k in range(count)], axis=1
                        ))
                parts.append(jnp.dot(
                    up_w[rp, cp], jnp.concatenate(pieces, axis=0), preferred_element_type=f32
                ).astype(bf16))
            for k in range(count):
                cut = slice(k * width, (k + 1) * width)
                both = jnp.concatenate([parts[0][:, cut], parts[1][:, cut]], axis=1)
                mixed = jnp.dot(both, perm[...], preferred_element_type=f32)
                for h in range(2):
                    value = mixed[:, h * width:(h + 1) * width]
                    r = 2 * (start + k + h * apart) - 2 + rp
                    if 2 <= r < 2 * rows + 2:
                        ups[r - 2] = value.astype(bf16)
                    act = activate(value, gains[0])
                    if r < 2:
                        act = jnp.where(has_above, act, 0.0)
                    if r >= 2 * rows + 2:
                        act = jnp.where(has_below, act, 0.0)
                    place(first, r, act.astype(bf16), n)

    def windows(field3, start, count):
        return jnp.concatenate(
            [field3[pl.ds(start + k, 3)].reshape(9 * chans, width) for k in range(count)], axis=1
        )

    def conv_one(start, count, n):
        total = jnp.dot(one_w[...], windows(first, start, count), preferred_element_type=f32)
        total = total.astype(bf16).astype(f32)
        for k in range(count):
            r = start + k
            act = activate(total[:, k * width:(k + 1) * width], gains[1])
            if r == 0:
                act = jnp.where(has_above, act, 0.0)
            if r == 2 * rows + 1:
                act = jnp.where(has_below, act, 0.0)
            place(second, r, act.astype(bf16), n)

    writes = []

    def conv_two(start, count):
        total = jnp.dot(two_w[...], windows(second, start, count), preferred_element_type=f32)
        for k in range(count):
            value = total[:, k * width:(k + 1) * width] + ups[start + k].astype(f32)
            obuf[start + k] = value.astype(bf16)
        item = pltpu.make_async_copy(
            obuf.at[pl.ds(start, count)], out.at[0, pl.ds(start, count)],
            done.at[len(writes)],
        )
        item.start()
        writes.append(item)

    edges[...] = jnp.zeros(edges.shape, bf16)
    own.wait()
    side.wait()
    inner = rows // 2 - 1
    for k in range(inner + 2):
        make_pair(k, 2 + k, inner)
    for item in up_copies:
        item.wait()
    upsample(0, inner, 3, inner, 0)

    @pl.when(has_above)
    def _():
        down.wait_recv()
        pass_top.start()

    @pl.when(has_below)
    def _():
        up.wait_recv()
        pass_bottom.start()

    swaps[0].start()

    @pl.when(has_above)
    def _():
        up.wait_send()
        pass_top.wait()

    @pl.when(has_below)
    def _():
        down.wait_send()
        pass_bottom.wait()

    for k in range(4):
        make_pair(inner + 2 + k, k, rows)
    upsample(inner + 2, 2, 1, rows, 1)

    swaps[0].wait()
    for r in range(4, 2 * rows):
        join(first, r, 0)
    swaps[1].start()
    last = 2 * rows - 2
    conv_one(4, 4, 2)
    conv_one(8, 4, 2)
    conv_one(12, last - 12, 2)
    swaps[1].wait()
    for r in (*range(4), *range(2 * rows, 2 * rows + 4)):
        join(first, r, 1)
    swaps[2].start()
    conv_one(0, 4, 3)
    conv_one(last, 4, 3)
    swaps[2].wait()
    for r in range(4, last):
        join(second, r, 2)
    swaps[3].start()
    conv_two(4, 4)
    conv_two(8, 4)
    swaps[3].wait()
    for r in (*range(4), *range(last, last + 4)):
        join(second, r, 3)
    conv_two(0, 4)
    conv_two(12, 4)
    for item in writes:
        item.wait()


def local(ha_count, latent, up_weight, conv_one, gain_one, conv_two, gain_two):
    _, rows, width, share = latent.shape
    chans = conv_one.shape[3]
    latent = jnp.transpose(latent, (0, 1, 3, 2))
    up_weight = jnp.transpose(up_weight, (0, 1, 3, 2))
    anywhere = pl.BlockSpec(memory_space=pl.ANY)
    vmem = pl.BlockSpec(memory_space=pltpu.VMEM)
    depth = 2 * share
    result = pl.pallas_call(
        functools.partial(block_kernel, ha_count),
        out_shape=jax.ShapeDtypeStruct((1, 2 * rows, chans, width), bf16),
        in_specs=[anywhere] + [vmem] * 2 + [anywhere] * 3,
        out_specs=anywhere,
        scratch_shapes=[
            pltpu.VMEM((2, 2, chans, 4 * depth), bf16),
            pltpu.VMEM((2, 3, 3, chans, chans), bf16),
            pltpu.VMEM((chans, 9 * chans), bf16),
            pltpu.VMEM((chans, 9 * chans), bf16),
            pltpu.VMEM((rows + 4, depth, width), bf16),
            pltpu.VMEM((rows // 2 + 5, 3, depth, width), bf16),
            pltpu.VMEM((2 * rows, chans, width), bf16),
            pltpu.VMEM((2 * rows + 4, 3 * chans, width), bf16),
            pltpu.VMEM((2 * rows + 2, 3 * chans, width), bf16),
            pltpu.VMEM((2, chans, width), f32),
            pltpu.VMEM((2 * width, 2 * width), bf16),
            pltpu.VMEM((4, chans, width), bf16),
            pltpu.VMEM((4, chans, width), bf16),
            pltpu.VMEM((2 * rows, chans, width), bf16),
            pltpu.SemaphoreType.DMA((4,)),
            pltpu.SemaphoreType.DMA((9,)),
            pltpu.SemaphoreType.DMA((9,)),
            pltpu.SemaphoreType.DMA((4,)),
        ],
        compiler_params=pltpu.CompilerParams(
            vmem_limit_bytes=60000 * 1024, collective_id=0, has_side_effects=True
        ),
    )(latent, gain_one.reshape(1, chans), gain_two.reshape(1, chans),
      up_weight, conv_one, conv_two)
    return jnp.transpose(result, (0, 1, 3, 2))


def solution(mesh):
    return jax.shard_map(
        functools.partial(local, mesh.shape["ha"]),
        mesh=mesh,
        in_specs=(P("grp", "ha", None, "col"), P(), P(), P(), P(), P()),
        out_specs=P("grp", "ha", "col", None),
        check_vma=False,
    )
```

```python
import functools

import jax
import jax.numpy as jnp
from jax import lax
from jax.experimental import pallas as pl
from jax.experimental.pallas import tpu as pltpu
from jax.sharding import PartitionSpec as P

f32 = jnp.float32
bf16 = jnp.bfloat16
MESH = pl.DeviceIdType.MESH
SLOT = 8
SLOT_AT = 3
phase_taps = (((0, 1), (-1, 3)), ((0, 2), (1, 0)))


def activate(wide, half_gain):
    stats = jnp.sum(wide * wide, axis=0, keepdims=True) * (1.0 / wide.shape[0])
    half = wide * lax.rsqrt(stats + 1e-06) * half_gain
    return half * jnp.tanh(half) + half


def block_kernel(
    ha_count, lat, gain_one, gain_two, up_hbm, one_hbm, two_hbm, out,
    up_w, raw, one_w, two_w, field, pairs, ups, first, second, gains, perm,
    edges, halos, sem, send, recv
):
    ha = lax.axis_index("ha")
    col = lax.axis_index("col")
    rows, share, width = lat.shape[1], lat.shape[2], lat.shape[3]
    chans = out.shape[2]
    half = width // 2
    depth = 2 * share
    mine = pl.ds(pl.multiple_of(col * share, share), share)
    other = {"col": 1 - col}
    has_above, has_below = ha > 0, ha < ha_count - 1

    barrier = pltpu.get_barrier_semaphore()
    pl.semaphore_signal(barrier, 1, device_id=other, device_id_type=MESH)

    @pl.when(has_above)
    def _():
        pl.semaphore_signal(barrier, 1, device_id={"ha": ha - 1}, device_id_type=MESH)

    @pl.when(has_below)
    def _():
        pl.semaphore_signal(barrier, 1, device_id={"ha": ha + 1}, device_id_type=MESH)

    own = pltpu.make_async_copy(lat.at[0], field.at[pl.ds(2, rows), mine], sem.at[0])
    own.start()
    raw_copies = [
        pltpu.make_async_copy(src, raw.at[n], sem.at[1 + n])
        for n, src in enumerate((one_hbm, two_hbm))
    ]
    for item in raw_copies:
        item.start()
    up_copies = []
    for rp in range(2):
        for cp in range(2):
            tap = 0
            for _, ra in phase_taps[rp]:
                for _, cb in phase_taps[cp]:
                    up_copies.append(pltpu.make_async_copy(
                        up_hbm.at[ra, cb],
                        up_w.at[rp, cp, :, pl.ds(tap * depth, depth)],
                        sem.at[3],
                    ))
                    tap += 1
    for item in up_copies:
        item.start()

    peers = 1 + jnp.minimum(ha, 1) + jnp.minimum(ha_count - 1 - ha, 1)
    pl.semaphore_wait(barrier, peers)

    def remote(src, dst, target, n):
        return pltpu.make_async_remote_copy(
            src_ref=src, dst_ref=dst, send_sem=send.at[n], recv_sem=recv.at[n],
            device_id=target, device_id_type=MESH,
        )

    side = remote(lat.at[0], field.at[pl.ds(2, rows), mine], other, 0)
    downs, ups_sent, pass_tops, pass_bottoms = [], [], [], []
    for n in range(2):
        top, bottom = field.at[1 - n, mine], field.at[rows + 2 + n, mine]
        downs.append(remote(lat.at[0, rows - 1 - n], top, {"ha": ha + 1}, 1 + n))
        ups_sent.append(remote(lat.at[0, n], bottom, {"ha": ha - 1}, 3 + n))
        pass_tops.append(remote(top, top, other, 5 + n))
        pass_bottoms.append(remote(bottom, bottom, other, 7 + n))
    swaps = [remote(edges.at[n], halos.at[n], other, 9 + n) for n in range(3)]

    for n in range(2):
        @pl.when(has_below)
        def _():
            downs[n].start()

        @pl.when(has_above)
        def _():
            ups_sent[n].start()

    side.start()

    @pl.when(ha == 0)
    def _():
        field[pl.ds(0, 2)] = jnp.zeros((2, depth, width), bf16)

    @pl.when(ha == ha_count - 1)
    def _():
        field[pl.ds(rows + 2, 2)] = jnp.zeros((2, depth, width), bf16)

    for n, gain in enumerate((gain_one, gain_two)):
        gains[n] = jnp.broadcast_to(gain[...] * 0.5, (width, chans)).T
    at = lax.broadcasted_iota(jnp.int32, (2 * width, 2 * width), 0)
    to = lax.broadcasted_iota(jnp.int32, (2 * width, 2 * width), 1)
    source = (to % 2) * width + (to // width) * half + (to % width) // 2
    perm[...] = (source == at).astype(f32).astype(bf16)
    edges[...] = jnp.zeros(edges.shape, bf16)

    def turn(n, turned):
        at = lax.broadcasted_iota(jnp.int32, (chans, chans), 0)
        to = lax.broadcasted_iota(jnp.int32, (chans, chans), 1)
        eye = (at == to).astype(f32).astype(bf16)
        taps = [raw[n, a, b] for a in range(3) for b in (2 - 2 * col, 1, 2 * col)]
        turned[...] = lax.dot_general(
            eye, jnp.concatenate(taps, axis=0), (((1,), (1,)), ((), ())),
            preferred_element_type=f32,
        ).astype(bf16)

    lane = lax.broadcasted_iota(jnp.int32, (share, width), 1)
    keep_near = (lane < half) == (col == 0)
    low = lane % half == 0
    high = lane % half == half - 1
    low_col = low & (col == 0)
    high_col = high & (col > 0)
    zero = jnp.zeros((share, width), bf16)

    def store_planes(n, here, there, part):
        pairs[n, 1, part] = here
        pairs[n, 0, part] = pltpu.roll(
            jnp.where(high_col, there, jnp.where(high, zero, here)), 1, 1
        )
        pairs[n, 2, part] = pltpu.roll(
            jnp.where(low_col, there, jnp.where(low, zero, here)), width - 1, 1
        )

    def halves(f, apart, part):
        near = field[f + apart * col, part]
        far = pltpu.roll(field[f + apart * (1 - col), part], half, 1)
        return jnp.where(keep_near, near, far), jnp.where(keep_near, far, near)

    def make_pair(n, f, apart, part):
        here, there = halves(f, apart, part)
        store_planes(n, here, there, part)

    def halo_slots(listed, part):
        total = zero
        for s, f in enumerate(listed):
            moved = pltpu.roll(field[f, part], SLOT * s + SLOT_AT + col, 1)
            total = jnp.where(lane // SLOT == half // SLOT + s, moved, total)
        return total

    cell = lax.broadcasted_iota(jnp.int32, (chans, width), 1)
    blank = jnp.zeros((chans, width), bf16)
    inward = 1 + (1 - col) * (width - 2)
    outward = 1 + col * (width - 2)
    joint_cell = cell == (1 - col) * (width - 1)
    rim_cell = cell == col * (width - 1)

    def place(field3, r, value, moved):
        turned_in = pltpu.roll(value, inward, 1)
        if moved is not None:
            turned_in = jnp.where(joint_cell, moved, turned_in)
        field3[r, pl.ds(chans, chans)] = value
        field3[r, pl.ds(0, chans)] = turned_in
        field3[r, pl.ds(2 * chans, chans)] = jnp.where(
            rim_cell, blank, pltpu.roll(value, outward, 1)
        )

    def join(field3, span, n):
        for r in span:
            moved = pltpu.roll(halos[n], width - 2 - r + col, 1)
            field3[r, pl.ds(0, chans)] = jnp.where(
                joint_cell, moved, field3[r, pl.ds(0, chans)]
            )

    def framed(r, value):
        if r < 2:
            return jnp.where(has_above, value, jnp.zeros_like(value))
        if r >= 2 * rows + 2:
            return jnp.where(has_below, value, jnp.zeros_like(value))
        return value

    def upsample(plane, count, plan):
        for rp in range(2):
            parts = []
            for cp in range(2):
                pieces = [
                    jnp.concatenate([plane(rp, k, dr + 1 - rp, dc) for k in range(count)], axis=1)
                    for dr, _ in phase_taps[rp] for dc, _ in phase_taps[cp]
                ]
                parts.append(jnp.dot(
                    up_w[rp, cp], jnp.concatenate(pieces, axis=0), preferred_element_type=f32
                ).astype(bf16))
            extra = None
            for k in (count - 1, *range(count - 1)):
                cut = slice(k * width, (k + 1) * width)
                both = jnp.concatenate([parts[0][:, cut], parts[1][:, cut]], axis=1)
                mixed = jnp.dot(both, perm[...], preferred_element_type=f32)
                todo = plan(rp, k)
                for side_half in sorted(range(2), key=lambda x: todo[x] != "halo"):
                    value = mixed[:, side_half * width:(side_half + 1) * width]
                    act = activate(value, gains[0]).astype(bf16)
                    if todo[side_half] == "halo":
                        extra = act
                        continue
                    r, slot = todo[side_half]
                    if 2 <= r < 2 * rows + 2:
                        ups[r - 2] = value.astype(bf16)
                    moved = pltpu.roll(extra, width - 1 - 2 * SLOT_AT - 2 * SLOT * slot, 1)
                    place(first, r, framed(r, act), framed(r, moved))

    def windows(field3, span):
        return jnp.concatenate(
            [field3[pl.ds(r, 3)].reshape(9 * chans, width) for r in span], axis=1
        )

    def conv_one(span, n):
        total = jnp.dot(one_w[...], windows(first, span), preferred_element_type=f32)
        total = total.astype(bf16).astype(f32)
        for k, r in enumerate(span):
            act = activate(total[:, k * width:(k + 1) * width], gains[1])
            if r == 0:
                act = jnp.where(has_above, act, 0.0)
            if r == 2 * rows + 1:
                act = jnp.where(has_below, act, 0.0)
            act = act.astype(bf16)
            place(second, r, act, None)
            edges[n] = jnp.where(cell == r + 1, pltpu.roll(act, r + 2 - col, 1), edges[n])

    def conv_two(span):
        total = jnp.dot(two_w[...], windows(second, span), preferred_element_type=f32)
        for k, r in enumerate(span):
            value = total[:, k * width:(k + 1) * width] + ups[r].astype(f32)
            out[0, r] = value.astype(bf16)

    def forward(n):
        @pl.when(has_above)
        def _():
            downs[n].wait_recv()
            pass_tops[n].start()

        @pl.when(has_below)
        def _():
            ups_sent[n].wait_recv()
            pass_bottoms[n].start()

    def arrived(n):
        @pl.when(has_above)
        def _():
            ups_sent[n].wait_send()
            pass_tops[n].wait()

        @pl.when(has_below)
        def _():
            downs[n].wait_send()
            pass_bottoms[n].wait()

    h = rows // 2
    theirs = pl.ds(pl.multiple_of((1 - col) * share, share), share)
    base = h + 2

    def inner_pairs(part):
        for k in range(h):
            make_pair(k, 2 + k, h, part)
        slots = halo_slots(range(2, rows + 2), part)
        for k in range(2):
            here, there = halves(1 + h + k, 0, part)
            here = jnp.where(lane < half, here, slots)
            store_planes(h + k, here, there, part)
            slots = pltpu.roll(slots, width - SLOT, 1)

    def inner_plane(rp, k, step, dc):
        return pairs[k + step if k < h - 1 else h + step, 1 + dc]

    def inner_plan(rp, k):
        r = 4 - rp + 2 * k
        if k == h - 1:
            return (r, k), "halo"
        return (r, k), (r + 2 * h, k + h)

    def outer_pairs(part):
        for k in range(3):
            make_pair(base + k, k, rows + 1, part)
        slots = halo_slots((0, 1, 2, rows + 1, rows + 2, rows + 3), part)
        slots = jnp.where(lane < half, pltpu.roll(slots, half, 1), slots)
        for k in range(2):
            store_planes(base + 3 + k, slots, slots, part)
            slots = pltpu.roll(slots, width - SLOT, 1)

    full_lane = lax.broadcasted_iota(jnp.int32, (depth, width), 1) < half

    def outer_plane(rp, k, step, dc):
        if k == 0:
            return pairs[base + rp + step, 1 + dc]
        slots = pairs[base + 3 + step, 1 + dc]
        if rp == 0:
            return jnp.where(full_lane, pairs[base + 1 + step, 1 + dc], slots)
        return jnp.where(full_lane, slots, pairs[base + step, 1 + dc])

    def outer_plan(rp, k):
        if k == 0:
            return (rp, rp), (2 * rows + 2 + rp, 3 + rp)
        return ((2, 1), "halo") if rp == 0 else ("halo", (2 * rows + 1, 3))

    own.wait()
    inner_pairs(mine)
    for n, turned in enumerate((one_w, two_w)):
        raw_copies[n].wait()
        turn(n, turned)
    side.wait()
    inner_pairs(theirs)
    for item in up_copies:
        item.wait()
    upsample(inner_plane, h, inner_plan)
    conv_one(range(3, 7), 0)
    conv_one(range(7, 11), 0)
    swaps[0].start()
    forward(0)
    conv_one(range(11, 2 * rows - 1), 1)
    swaps[1].start()
    forward(1)
    swaps[0].wait()
    join(second, range(3, 11), 0)
    conv_two(range(3, 7))
    conv_two(range(7, 9))
    arrived(0)
    arrived(1)
    outer_pairs(pl.ds(0, share))
    outer_pairs(pl.ds(share, share))
    upsample(outer_plane, 2, outer_plan)
    conv_one((0, 1, 2, 2 * rows - 1), 2)
    conv_one((2 * rows, 2 * rows + 1), 2)
    swaps[2].start()
    swaps[1].wait()
    join(second, range(11, 2 * rows - 1), 1)
    conv_two(range(9, 2 * rows - 3))
    swaps[2].wait()
    join(second, (0, 1, 2, 2 * rows - 1, 2 * rows, 2 * rows + 1), 2)
    conv_two((0, 1, 2, 2 * rows - 3))
    conv_two((2 * rows - 2, 2 * rows - 1))


def finish_kernel(src, dst, sem):
    item = pltpu.make_async_copy(src, dst, sem.at[0])
    item.start()
    item.wait()


def local(ha_count, latent, up_weight, conv_one, gain_one, conv_two, gain_two):
    _, rows, width, share = latent.shape
    chans = conv_one.shape[3]
    latent = jnp.transpose(latent, (0, 1, 3, 2))
    up_weight = jnp.transpose(up_weight, (0, 1, 3, 2))
    anywhere = pl.BlockSpec(memory_space=pl.ANY)
    vmem = pl.BlockSpec(memory_space=pltpu.VMEM)
    depth = 2 * share
    result = pl.pallas_call(
        functools.partial(block_kernel, ha_count),
        out_shape=pltpu.VMEM((1, 2 * rows, chans, width), bf16),
        in_specs=[anywhere] + [vmem] * 2 + [anywhere] * 3,
        out_specs=vmem,
        scratch_shapes=[
            pltpu.VMEM((2, 2, chans, 4 * depth), bf16),
            pltpu.VMEM((2, 3, 3, chans, chans), bf16),
            pltpu.VMEM((chans, 9 * chans), bf16),
            pltpu.VMEM((chans, 9 * chans), bf16),
            pltpu.VMEM((rows + 4, depth, width), bf16),
            pltpu.VMEM((rows // 2 + 7, 3, depth, width), bf16),
            pltpu.VMEM((2 * rows, chans, width), bf16),
            pltpu.VMEM((2 * rows + 4, 3 * chans, width), bf16),
            pltpu.VMEM((2 * rows + 2, 3 * chans, width), bf16),
            pltpu.VMEM((2, chans, width), f32),
            pltpu.VMEM((2 * width, 2 * width), bf16),
            pltpu.VMEM((3, chans, width), bf16),
            pltpu.VMEM((3, chans, width), bf16),
            pltpu.SemaphoreType.DMA((4,)),
            pltpu.SemaphoreType.DMA((12,)),
            pltpu.SemaphoreType.DMA((12,)),
        ],
        compiler_params=pltpu.CompilerParams(
            vmem_limit_bytes=60000 * 1024, collective_id=0, has_side_effects=True
        ),
    )(latent, gain_one.reshape(1, chans), gain_two.reshape(1, chans),
      up_weight, conv_one, conv_two)
    result = pl.pallas_call(
        finish_kernel,
        out_shape=jax.ShapeDtypeStruct(result.shape, bf16),
        in_specs=[vmem],
        out_specs=pl.BlockSpec(memory_space=pltpu.HBM),
        scratch_shapes=[pltpu.SemaphoreType.DMA((1,))],
        compiler_params=pltpu.CompilerParams(vmem_limit_bytes=2 * 1024 * 1024),
    )(result)
    return jnp.transpose(result, (0, 1, 3, 2))


def solution(mesh):
    return jax.shard_map(
        functools.partial(local, mesh.shape["ha"]),
        mesh=mesh,
        in_specs=(P("grp", "ha", None, "col"), P(), P(), P(), P(), P()),
        out_specs=P("grp", "ha", "col", None),
        check_vma=False,
    )
```

```python
import functools

import jax
import jax.numpy as jnp
from jax import lax
from jax.experimental import pallas as pl
from jax.experimental.pallas import tpu as pltpu
from jax.sharding import PartitionSpec as P

f32 = jnp.float32
bf16 = jnp.bfloat16
MESH = pl.DeviceIdType.MESH
SLOT = 8
SLOT_AT = 3
phase_taps = (((0, 1), (-1, 3)), ((0, 2), (1, 0)))


def activate(wide, half_gain):
    stats = jnp.sum(wide * wide, axis=0, keepdims=True) * (1.0 / wide.shape[0])
    half = wide * lax.rsqrt(stats + 1e-06) * half_gain
    return half * jnp.tanh(half) + half


def block_kernel(
    ha_count, lat, gain_one, gain_two, up_hbm, one_hbm, two_hbm, out,
    up_w, raw, one_w, two_w, field, pairs, ups, first, second, gains, perm,
    slim, sem, send, recv
):
    ha = lax.axis_index("ha")
    col = lax.axis_index("col")
    rows, share, width = lat.shape[1], lat.shape[2], lat.shape[3]
    chans = out.shape[2]
    half = width // 2
    depth = 2 * share
    mine = pl.ds(pl.multiple_of(col * share, share), share)
    other = {"col": 1 - col}
    has_above, has_below = ha > 0, ha < ha_count - 1

    barrier = pltpu.get_barrier_semaphore()
    pl.semaphore_signal(barrier, 1, device_id=other, device_id_type=MESH)

    @pl.when(has_above)
    def _():
        pl.semaphore_signal(barrier, 1, device_id={"ha": ha - 1}, device_id_type=MESH)

    @pl.when(has_below)
    def _():
        pl.semaphore_signal(barrier, 1, device_id={"ha": ha + 1}, device_id_type=MESH)

    own = pltpu.make_async_copy(lat.at[0], field.at[pl.ds(2, rows), mine], sem.at[0])
    own.start()
    raw_copies = [
        pltpu.make_async_copy(src, raw.at[n], sem.at[1 + n])
        for n, src in enumerate((one_hbm, two_hbm))
    ]
    for item in raw_copies:
        item.start()
    up_copies = []
    for rp in range(2):
        for cp in range(2):
            tap = 0
            for _, ra in phase_taps[rp]:
                for _, cb in phase_taps[cp]:
                    up_copies.append(pltpu.make_async_copy(
                        up_hbm.at[ra, cb],
                        up_w.at[rp, cp, :, pl.ds(tap * depth, depth)],
                        sem.at[3],
                    ))
                    tap += 1
    for item in up_copies:
        item.start()

    for n, gain in enumerate((gain_one, gain_two)):
        gains[n] = jnp.broadcast_to(gain[...] * 0.5, (width, chans)).T
    at = lax.broadcasted_iota(jnp.int32, (2 * width, 2 * width), 0)
    to = lax.broadcasted_iota(jnp.int32, (2 * width, 2 * width), 1)
    source = (to % 2) * width + (to // width) * half + (to % width) // 2
    perm[...] = (source == at).astype(f32).astype(bf16)

    peers = 1 + jnp.minimum(ha, 1) + jnp.minimum(ha_count - 1 - ha, 1)
    pl.semaphore_wait(barrier, peers)

    def remote(src, dst, target, n):
        return pltpu.make_async_remote_copy(
            src_ref=src, dst_ref=dst, send_sem=send.at[n], recv_sem=recv.at[n],
            device_id=target, device_id_type=MESH,
        )

    side = remote(lat.at[0], field.at[pl.ds(2, rows), mine], other, 0)
    downs, ups_sent, pass_tops, pass_bottoms = [], [], [], []
    for n in range(2):
        top, bottom = field.at[1 - n, mine], field.at[rows + 2 + n, mine]
        downs.append(remote(lat.at[0, rows - 1 - n], top, {"ha": ha + 1}, 1 + n))
        ups_sent.append(remote(lat.at[0, n], bottom, {"ha": ha - 1}, 3 + n))
        pass_tops.append(remote(top, top, other, 5 + n))
        pass_bottoms.append(remote(bottom, bottom, other, 7 + n))

    for n in range(2):
        @pl.when(has_below)
        def _():
            downs[n].start()

        @pl.when(has_above)
        def _():
            ups_sent[n].start()

    side.start()

    @pl.when(ha == 0)
    def _():
        field[pl.ds(0, 2)] = jnp.zeros((2, depth, width), bf16)

    @pl.when(ha == ha_count - 1)
    def _():
        field[pl.ds(rows + 2, 2)] = jnp.zeros((2, depth, width), bf16)

    def turn(n, turned):
        at = lax.broadcasted_iota(jnp.int32, (chans, chans), 0)
        to = lax.broadcasted_iota(jnp.int32, (chans, chans), 1)
        eye = (at == to).astype(f32).astype(bf16)
        taps = [raw[n, a, b] for a in range(3) for b in (2 - 2 * col, 1, 2 * col)]
        turned[...] = lax.dot_general(
            eye, jnp.concatenate(taps, axis=0), (((1,), (1,)), ((), ())),
            preferred_element_type=f32,
        ).astype(bf16)

    lane = lax.broadcasted_iota(jnp.int32, (share, width), 1)
    keep_near = (lane < half) == (col == 0)
    low = lane % half == 0
    high = lane % half == half - 1
    low_col = low & (col == 0)
    high_col = high & (col > 0)
    zero = jnp.zeros((share, width), bf16)

    def store_planes(n, here, there, part):
        pairs[n, 1, part] = here
        pairs[n, 0, part] = pltpu.roll(
            jnp.where(high_col, there, jnp.where(high, zero, here)), 1, 1
        )
        pairs[n, 2, part] = pltpu.roll(
            jnp.where(low_col, there, jnp.where(low, zero, here)), width - 1, 1
        )

    def halves(f, apart, part):
        near = field[f + apart * col, part]
        far = pltpu.roll(field[f + apart * (1 - col), part], half, 1)
        return jnp.where(keep_near, near, far), jnp.where(keep_near, far, near)

    def make_pair(n, f, apart, part):
        here, there = halves(f, apart, part)
        store_planes(n, here, there, part)

    def halo_slots(listed, part):
        total = zero
        for s, f in enumerate(listed):
            moved = pltpu.roll(field[f, part], SLOT * s + SLOT_AT + col, 1)
            total = jnp.where(lane // SLOT == half // SLOT + s, moved, total)
        return total

    cell = lax.broadcasted_iota(jnp.int32, (chans, width), 1)
    blank = jnp.zeros((chans, width), bf16)
    inward = 1 + (1 - col) * (width - 2)
    outward = 1 + col * (width - 2)
    joint_cell = cell == (1 - col) * (width - 1)
    rim_cell = cell == col * (width - 1)

    def place(field3, r, value, moved):
        turned_in = pltpu.roll(value, inward, 1)
        if moved is not None:
            turned_in = jnp.where(joint_cell, moved, turned_in)
        field3[r, pl.ds(chans, chans)] = value
        field3[r, pl.ds(0, chans)] = turned_in
        field3[r, pl.ds(2 * chans, chans)] = jnp.where(
            rim_cell, blank, pltpu.roll(value, outward, 1)
        )

    def framed(r, value):
        if r < 2:
            return jnp.where(has_above, value, jnp.zeros_like(value))
        if r >= 2 * rows + 2:
            return jnp.where(has_below, value, jnp.zeros_like(value))
        return value

    def upsample(plane, count, plan):
        extras = []
        for rp in range(2):
            parts = []
            for cp in range(2):
                pieces = [
                    jnp.concatenate([plane(rp, k, dr + 1 - rp, dc) for k in range(count)], axis=1)
                    for dr, _ in phase_taps[rp] for dc, _ in phase_taps[cp]
                ]
                parts.append(jnp.dot(
                    up_w[rp, cp], jnp.concatenate(pieces, axis=0), preferred_element_type=f32
                ).astype(bf16))
            extra = None
            for k in (count - 1, *range(count - 1)):
                cut = slice(k * width, (k + 1) * width)
                both = jnp.concatenate([parts[0][:, cut], parts[1][:, cut]], axis=1)
                mixed = jnp.dot(both, perm[...], preferred_element_type=f32)
                todo = plan(rp, k)
                for side_half in sorted(range(2), key=lambda x: todo[x] != "halo"):
                    value = mixed[:, side_half * width:(side_half + 1) * width]
                    act = activate(value, gains[0]).astype(bf16)
                    if todo[side_half] == "halo":
                        extra = act
                        continue
                    r, slot = todo[side_half]
                    if 2 <= r < 2 * rows + 2:
                        ups[r - 2] = value.astype(bf16)
                    moved = pltpu.roll(extra, width - 1 - 2 * SLOT_AT - 2 * SLOT * slot, 1)
                    place(first, r, framed(r, act), framed(r, moved))
            extras.append(extra)
        return extras

    def windows(field3, span):
        return jnp.concatenate(
            [field3[pl.ds(r, 3)].reshape(9 * chans, width) for r in span], axis=1
        )

    def slim_near_far(first_half, second_half, apart):
        return [
            jnp.where(
                cell % (2 * SLOT) == SLOT - 1,
                pltpu.roll(first_half, shift, 1),
                pltpu.roll(second_half, apart + shift, 1),
            )
            for shift in (col, 1 - col)
        ]

    def slim_edges(listed):
        total = blank
        for r, s in listed:
            moved = pltpu.roll(first[r, pl.ds(chans, chans)], SLOT * s + SLOT - col, 1)
            total = jnp.where(cell // SLOT == s, moved, total)
        return total

    def slim_windows(slims):
        return jnp.concatenate(
            [pltpu.roll(x, (SLOT * (1 - d)) % width, 1) if d != 1 else x
             for d in range(3) for x in slims], axis=0
        )

    def normed(total):
        return activate(total.astype(bf16).astype(f32), gains[1])

    def conv_one(span, slims, slot_of):
        tops = [
            jnp.dot(one_w[...], windows(first, group), preferred_element_type=f32)
            for group in span[:1]
        ]
        joint = normed(
            jnp.dot(one_w[...], slim_windows(slims), preferred_element_type=f32)
        ).astype(bf16)
        for group in span[1:]:
            tops.append(jnp.dot(one_w[...], windows(first, group), preferred_element_type=f32))
        for group, total in zip(span, tops):
            for k, r in enumerate(group):
                act = normed(total[:, k * width:(k + 1) * width]).astype(bf16)
                moved = pltpu.roll(joint, width - SLOT * (slot_of(r) + 1) + col, 1)
                if r == 0 or r == 2 * rows + 1:
                    inside = has_above if r == 0 else has_below
                    act = jnp.where(inside, act, blank)
                    moved = jnp.where(inside, moved, blank)
                place(second, r, act, moved)

    def conv_two(span):
        total = jnp.dot(two_w[...], windows(second, span), preferred_element_type=f32)
        for k, r in enumerate(span):
            value = total[:, k * width:(k + 1) * width] + ups[r].astype(f32)
            out[0, r] = value.astype(bf16)

    def forward(n):
        @pl.when(has_above)
        def _():
            downs[n].wait_recv()
            pass_tops[n].start()

        @pl.when(has_below)
        def _():
            ups_sent[n].wait_recv()
            pass_bottoms[n].start()

    def arrived(n):
        @pl.when(has_above)
        def _():
            ups_sent[n].wait_send()
            pass_tops[n].wait()

        @pl.when(has_below)
        def _():
            downs[n].wait_send()
            pass_bottoms[n].wait()

    h = rows // 2
    theirs = pl.ds(pl.multiple_of((1 - col) * share, share), share)
    base = h + 2

    def inner_pairs(part):
        for k in range(h):
            make_pair(k, 2 + k, h, part)
        slots = halo_slots(range(2, rows + 2), part)
        for k in range(2):
            here, there = halves(1 + h + k, 0, part)
            here = jnp.where(lane < half, here, slots)
            store_planes(h + k, here, there, part)
            slots = pltpu.roll(slots, width - SLOT, 1)

    def inner_plane(rp, k, step, dc):
        return pairs[k + step if k < h - 1 else h + step, 1 + dc]

    def inner_plan(rp, k):
        r = 4 - rp + 2 * k
        if k == h - 1:
            return (r, k), "halo"
        return (r, k), (r + 2 * h, k + h)

    def outer_pairs(part):
        for k in range(3):
            make_pair(base + k, k, rows + 1, part)
        slots = halo_slots((0, 1, 2, 2, rows + 1, rows + 2, rows + 3), part)
        slots = jnp.where(lane < half, pltpu.roll(slots, half, 1), slots)
        for k in range(2):
            store_planes(base + 3 + k, slots, slots, part)
            slots = pltpu.roll(slots, width - SLOT, 1)

    full_lane = lax.broadcasted_iota(jnp.int32, (depth, width), 1) < half

    def outer_plane(rp, k, step, dc):
        if k == 0:
            return pairs[base + rp + step, 1 + dc]
        slots = pairs[base + 3 + step, 1 + dc]
        if rp == 0:
            return jnp.where(full_lane, pairs[base + 1 + step, 1 + dc], slots)
        return jnp.where(full_lane, slots, pairs[base + step, 1 + dc])

    def outer_plan(rp, k):
        if k == 0:
            return (rp, rp), (2 * rows + 2 + rp, 4 + rp)
        return ((2, 1), "halo") if rp == 0 else ("halo", (2 * rows + 1, 4))

    own.wait()
    inner_pairs(mine)
    raw_copies[0].wait()
    turn(0, one_w)
    raw_copies[1].wait()
    side.wait()
    inner_pairs(theirs)
    for item in up_copies:
        item.wait()

    extras = upsample(inner_plane, h, inner_plan)
    slims = slim_near_far(extras[1], extras[0], SLOT)
    slims.append(slim_edges([(r, r - 3) for r in range(3, 2 * rows + 1)]))
    for n in range(3):
        slim[n] = slims[n]
    turn(1, two_w)
    conv_one(
        (range(3, 7), range(7, 11), range(11, 2 * rows - 1)), slims, lambda r: r - 2
    )
    forward(0)
    forward(1)
    outer_pairs(mine)
    conv_two(range(3, 7))
    conv_two(range(7, 9))
    arrived(0)
    arrived(1)
    outer_pairs(theirs)
    extras = upsample(outer_plane, 2, outer_plan)
    conv_two(range(9, 2 * rows - 3))
    slims = slim_near_far(extras[0], extras[1], width - SLOT)
    slims.append(slim_edges([
        *((r, r) for r in range(5)), *((2 * rows - 1 + r, 5 + r) for r in range(5))
    ]))
    spot = cell // SLOT
    gone = ((spot < 2) & (ha == 0)) | ((spot >= 8) & (ha == ha_count - 1))
    for n in range(2):
        value = jnp.where(gone, blank, slims[n])
        value = jnp.where(spot == 3, pltpu.roll(slim[n], 3 * SLOT, 1), value)
        value = jnp.where(spot == 4, pltpu.roll(slim[n], 3 * SLOT, 1), value)
        old = pltpu.roll(slim[n], width - (2 * rows - 9) * SLOT, 1)
        slims[n] = jnp.where((spot == 5) | (spot == 6), old, value)
    conv_one(
        ((0, 1, 2, 2 * rows - 1), (2 * rows, 2 * rows + 1)), slims,
        lambda r: r + 1 if r < 3 else r - (2 * rows - 7)
    )
    conv_two((0, 1, 2, 2 * rows - 3))
    conv_two((2 * rows - 2, 2 * rows - 1))


def finish_kernel(src, dst, sem):
    item = pltpu.make_async_copy(src, dst, sem.at[0])
    item.start()
    item.wait()


def local(ha_count, latent, up_weight, conv_one, gain_one, conv_two, gain_two):
    _, rows, width, share = latent.shape
    chans = conv_one.shape[3]
    latent = jnp.transpose(latent, (0, 1, 3, 2))
    up_weight = jnp.transpose(up_weight, (0, 1, 3, 2))
    anywhere = pl.BlockSpec(memory_space=pl.ANY)
    vmem = pl.BlockSpec(memory_space=pltpu.VMEM)
    depth = 2 * share
    result = pl.pallas_call(
        functools.partial(block_kernel, ha_count),
        out_shape=pltpu.VMEM((1, 2 * rows, chans, width), bf16),
        in_specs=[anywhere] + [vmem] * 2 + [anywhere] * 3,
        out_specs=vmem,
        scratch_shapes=[
            pltpu.VMEM((2, 2, chans, 4 * depth), bf16),
            pltpu.VMEM((2, 3, 3, chans, chans), bf16),
            pltpu.VMEM((chans, 9 * chans), bf16),
            pltpu.VMEM((chans, 9 * chans), bf16),
            pltpu.VMEM((rows + 4, depth, width), bf16),
            pltpu.VMEM((rows // 2 + 7, 3, depth, width), bf16),
            pltpu.VMEM((2 * rows, chans, width), bf16),
            pltpu.VMEM((2 * rows + 4, 3 * chans, width), bf16),
            pltpu.VMEM((2 * rows + 2, 3 * chans, width), bf16),
            pltpu.VMEM((2, chans, width), f32),
            pltpu.VMEM((2 * width, 2 * width), bf16),
            pltpu.VMEM((3, chans, width), bf16),
            pltpu.SemaphoreType.DMA((4,)),
            pltpu.SemaphoreType.DMA((9,)),
            pltpu.SemaphoreType.DMA((9,)),
        ],
        compiler_params=pltpu.CompilerParams(
            vmem_limit_bytes=60000 * 1024, collective_id=0, has_side_effects=True
        ),
    )(latent, gain_one.reshape(1, chans), gain_two.reshape(1, chans),
      up_weight, conv_one, conv_two)
    result = pl.pallas_call(
        finish_kernel,
        out_shape=jax.ShapeDtypeStruct(result.shape, bf16),
        in_specs=[vmem],
        out_specs=pl.BlockSpec(memory_space=pltpu.HBM),
        scratch_shapes=[pltpu.SemaphoreType.DMA((1,))],
        compiler_params=pltpu.CompilerParams(vmem_limit_bytes=2 * 1024 * 1024),
    )(result)
    return jnp.transpose(result, (0, 1, 3, 2))


def solution(mesh):
    return jax.shard_map(
        functools.partial(local, mesh.shape["ha"]),
        mesh=mesh,
        in_specs=(P("grp", "ha", None, "col"), P(), P(), P(), P(), P()),
        out_specs=P("grp", "ha", "col", None),
        check_vma=False,
    )
```

```python
import functools

import jax
import jax.numpy as jnp
from jax import lax
from jax.experimental import pallas as pl
from jax.experimental.pallas import tpu as pltpu
from jax.sharding import PartitionSpec as P

f32 = jnp.float32
bf16 = jnp.bfloat16
MESH = pl.DeviceIdType.MESH
SLOT = 8
SLOT_AT = 3
phase_taps = (((0, 1), (-1, 3)), ((0, 2), (1, 0)))


def activate(wide, half_gain):
    stats = jnp.sum(wide * wide, axis=0, keepdims=True) * (1.0 / wide.shape[0])
    half = wide * lax.rsqrt(stats + 1e-06) * half_gain
    return half * jnp.tanh(half) + half


def block_kernel(
    ha_count, lat, gain_one, gain_two, up_hbm, one_hbm, two_hbm, out, two_w, ups, second,
    up_w, raw, one_w, field, pairs, first, gains, perm,
    slim, sem, send, recv
):
    ha = lax.axis_index("ha")
    col = lax.axis_index("col")
    rows, share, width = lat.shape[1], lat.shape[2], lat.shape[3]
    chans = out.shape[2]
    half = width // 2
    depth = 2 * share
    mine = pl.ds(pl.multiple_of(col * share, share), share)
    other = {"col": 1 - col}
    has_above, has_below = ha > 0, ha < ha_count - 1

    barrier = pltpu.get_barrier_semaphore()
    pl.semaphore_signal(barrier, 1, device_id=other, device_id_type=MESH)

    @pl.when(has_above)
    def _():
        pl.semaphore_signal(barrier, 1, device_id={"ha": ha - 1}, device_id_type=MESH)

    @pl.when(has_below)
    def _():
        pl.semaphore_signal(barrier, 1, device_id={"ha": ha + 1}, device_id_type=MESH)

    own = pltpu.make_async_copy(lat.at[0], field.at[pl.ds(2, rows), mine], sem.at[0])
    own.start()
    raw_copies = [
        pltpu.make_async_copy(src, raw.at[n], sem.at[1 + n])
        for n, src in enumerate((one_hbm, two_hbm))
    ]
    for item in raw_copies:
        item.start()
    up_copies = []
    for rp in range(2):
        for cp in range(2):
            tap = 0
            for _, ra in phase_taps[rp]:
                for _, cb in phase_taps[cp]:
                    up_copies.append(pltpu.make_async_copy(
                        up_hbm.at[ra, cb],
                        up_w.at[rp, cp, :, pl.ds(tap * depth, depth)],
                        sem.at[3],
                    ))
                    tap += 1
    for item in up_copies:
        item.start()

    peers = 1 + jnp.minimum(ha, 1) + jnp.minimum(ha_count - 1 - ha, 1)
    pl.semaphore_wait(barrier, peers)

    def remote(src, dst, target, n):
        return pltpu.make_async_remote_copy(
            src_ref=src, dst_ref=dst, send_sem=send.at[n], recv_sem=recv.at[n],
            device_id=target, device_id_type=MESH,
        )

    side = remote(lat.at[0], field.at[pl.ds(2, rows), mine], other, 0)
    downs, ups_sent, pass_tops, pass_bottoms = [], [], [], []
    for n in range(2):
        top, bottom = field.at[1 - n, mine], field.at[rows + 2 + n, mine]
        downs.append(remote(lat.at[0, rows - 1 - n], top, {"ha": ha + 1}, 1 + n))
        ups_sent.append(remote(lat.at[0, n], bottom, {"ha": ha - 1}, 3 + n))
        pass_tops.append(remote(top, top, other, 5 + n))
        pass_bottoms.append(remote(bottom, bottom, other, 7 + n))

    for n in range(2):
        @pl.when(has_below)
        def _():
            downs[n].start()

        @pl.when(has_above)
        def _():
            ups_sent[n].start()

    side.start()

    @pl.when(ha == 0)
    def _():
        field[pl.ds(0, 2)] = jnp.zeros((2, depth, width), bf16)

    @pl.when(ha == ha_count - 1)
    def _():
        field[pl.ds(rows + 2, 2)] = jnp.zeros((2, depth, width), bf16)

    for n, gain in enumerate((gain_one, gain_two)):
        gains[n] = jnp.broadcast_to(gain[...] * 0.5, (width, chans)).T
    at = lax.broadcasted_iota(jnp.int32, (2 * width, 2 * width), 0)
    to = lax.broadcasted_iota(jnp.int32, (2 * width, 2 * width), 1)
    source = (to % 2) * width + (to // width) * half + (to % width) // 2
    perm[...] = (source == at).astype(f32).astype(bf16)

    def turn(n, turned):
        at = lax.broadcasted_iota(jnp.int32, (chans, chans), 0)
        to = lax.broadcasted_iota(jnp.int32, (chans, chans), 1)
        eye = (at == to).astype(f32).astype(bf16)
        taps = [raw[n, a, b] for a in range(3) for b in (2 - 2 * col, 1, 2 * col)]
        turned[...] = lax.dot_general(
            eye, jnp.concatenate(taps, axis=0), (((1,), (1,)), ((), ())),
            preferred_element_type=f32,
        ).astype(bf16)

    lane = lax.broadcasted_iota(jnp.int32, (share, width), 1)
    keep_near = (lane < half) == (col == 0)
    low = lane % half == 0
    high = lane % half == half - 1
    low_col = low & (col == 0)
    high_col = high & (col > 0)
    zero = jnp.zeros((share, width), bf16)

    def store_planes(n, here, there, part):
        pairs[n, 1, part] = here
        pairs[n, 0, part] = pltpu.roll(
            jnp.where(high_col, there, jnp.where(high, zero, here)), 1, 1
        )
        pairs[n, 2, part] = pltpu.roll(
            jnp.where(low_col, there, jnp.where(low, zero, here)), width - 1, 1
        )

    def halves(f, apart, part):
        near = field[f + apart * col, part]
        far = pltpu.roll(field[f + apart * (1 - col), part], half, 1)
        return jnp.where(keep_near, near, far), jnp.where(keep_near, far, near)

    def make_pair(n, f, apart, part):
        here, there = halves(f, apart, part)
        store_planes(n, here, there, part)

    def halo_slots(listed, part):
        total = zero
        for s, f in enumerate(listed):
            moved = pltpu.roll(field[f, part], SLOT * s + SLOT_AT + col, 1)
            total = jnp.where(lane // SLOT == half // SLOT + s, moved, total)
        return total

    cell = lax.broadcasted_iota(jnp.int32, (chans, width), 1)
    blank = jnp.zeros((chans, width), bf16)
    inward = 1 + (1 - col) * (width - 2)
    outward = 1 + col * (width - 2)
    joint_cell = cell == (1 - col) * (width - 1)
    rim_cell = cell == col * (width - 1)

    def place(field3, r, value, moved):
        turned_in = pltpu.roll(value, inward, 1)
        if moved is not None:
            turned_in = jnp.where(joint_cell, moved, turned_in)
        field3[r, pl.ds(chans, chans)] = value
        field3[r, pl.ds(0, chans)] = turned_in
        field3[r, pl.ds(2 * chans, chans)] = jnp.where(
            rim_cell, blank, pltpu.roll(value, outward, 1)
        )

    def framed(r, value):
        if r < 2:
            return jnp.where(has_above, value, jnp.zeros_like(value))
        if r >= 2 * rows + 2:
            return jnp.where(has_below, value, jnp.zeros_like(value))
        return value

    def upsample(plane, count, plan, apart):
        extras = []
        parts = {}

        def phase(rp, cp):
            pieces = [
                jnp.concatenate([plane(rp, k, dr + 1 - rp, dc) for k in range(count)], axis=1)
                for dr, _ in phase_taps[rp] for dc, _ in phase_taps[cp]
            ]
            parts[rp, cp] = jnp.dot(
                up_w[rp, cp], jnp.concatenate(pieces, axis=0), preferred_element_type=f32
            ).astype(bf16)

        if apart:
            for cp in range(2):
                for rp in range(2):
                    phase(rp, cp)
        for rp in range(2):
            if not apart:
                phase(rp, 0)
                phase(rp, 1)
            extra = None
            for k in (count - 1, *range(count - 1)):
                cut = slice(k * width, (k + 1) * width)
                both = jnp.concatenate([parts[rp, 0][:, cut], parts[rp, 1][:, cut]], axis=1)
                mixed = jnp.dot(both, perm[...], preferred_element_type=f32)
                todo = plan(rp, k)
                for side_half in sorted(range(2), key=lambda x: todo[x] != "halo"):
                    value = mixed[:, side_half * width:(side_half + 1) * width]
                    act = activate(value, gains[0]).astype(bf16)
                    if todo[side_half] == "halo":
                        extra = act
                        continue
                    r, slot = todo[side_half]
                    if 2 <= r < 2 * rows + 2:
                        ups[r - 2] = value.astype(bf16)
                    moved = pltpu.roll(extra, width - 1 - 2 * SLOT_AT - 2 * SLOT * slot, 1)
                    place(first, r, framed(r, act), framed(r, moved))
            extras.append(extra)
        return extras

    def windows(field3, span):
        return jnp.concatenate(
            [field3[pl.ds(r, 3)].reshape(9 * chans, width) for r in span], axis=1
        )

    def slim_near_far(first_half, second_half, apart):
        return [
            jnp.where(
                cell % (2 * SLOT) == SLOT - 1,
                pltpu.roll(first_half, shift, 1),
                pltpu.roll(second_half, apart + shift, 1),
            )
            for shift in (col, 1 - col)
        ]

    def slim_edges(listed):
        total = blank
        for r, s in listed:
            moved = pltpu.roll(first[r, pl.ds(chans, chans)], SLOT * s + SLOT - col, 1)
            total = jnp.where(cell // SLOT == s, moved, total)
        return total

    def slim_windows(slims):
        return jnp.concatenate(
            [pltpu.roll(x, (SLOT * (1 - d)) % width, 1) if d != 1 else x
             for d in range(3) for x in slims], axis=0
        )

    def normed(total):
        return activate(total.astype(bf16).astype(f32), gains[1])

    def conv_one(span, slims, slot_of):
        totals = {}
        for group in span:
            rhs = jnp.concatenate([
                slim_windows(slims) if r is None else
                first[pl.ds(r, 3)].reshape(9 * chans, width) for r in group
            ], axis=1)
            total = jnp.dot(one_w[...], rhs, preferred_element_type=f32)
            for k, r in enumerate(group):
                totals[r] = total[:, k * width:(k + 1) * width]
        joint = normed(totals[None]).astype(bf16)
        for group in span:
            for r in group:
                if r is None:
                    continue
                act = normed(totals[r]).astype(bf16)
                moved = pltpu.roll(joint, width - SLOT * (slot_of(r) + 1) + col, 1)
                if r == 0 or r == 2 * rows + 1:
                    inside = has_above if r == 0 else has_below
                    act = jnp.where(inside, act, blank)
                    moved = jnp.where(inside, moved, blank)
                place(second, r, act, moved)

    def conv_two(span):
        total = jnp.dot(two_w[...], windows(second, span), preferred_element_type=f32)
        for k, r in enumerate(span):
            value = total[:, k * width:(k + 1) * width] + ups[r].astype(f32)
            out[0, r] = value.astype(bf16)

    def forward(n):
        @pl.when(has_above)
        def _():
            downs[n].wait_recv()
            pass_tops[n].start()

        @pl.when(has_below)
        def _():
            ups_sent[n].wait_recv()
            pass_bottoms[n].start()

    def arrived(n):
        @pl.when(has_above)
        def _():
            ups_sent[n].wait_send()
            pass_tops[n].wait()

        @pl.when(has_below)
        def _():
            downs[n].wait_send()
            pass_bottoms[n].wait()

    h = rows // 2
    theirs = pl.ds(pl.multiple_of((1 - col) * share, share), share)
    base = h + 2

    def inner_pairs(part):
        for k in range(h):
            make_pair(k, 2 + k, h, part)
        slots = halo_slots(range(2, rows + 2), part)
        for k in range(2):
            here, there = halves(1 + h + k, 0, part)
            here = jnp.where(lane < half, here, slots)
            store_planes(h + k, here, there, part)
            slots = pltpu.roll(slots, width - SLOT, 1)

    def inner_plane(rp, k, step, dc):
        return pairs[k + step if k < h - 1 else h + step, 1 + dc]

    def inner_plan(rp, k):
        r = 4 - rp + 2 * k
        if k == h - 1:
            return (r, k), "halo"
        return (r, k), (r + 2 * h, k + h)

    def outer_pairs(part):
        for k in range(3):
            make_pair(base + k, k, rows + 1, part)
        slots = halo_slots((0, 1, 2, 2, rows + 1, rows + 2, rows + 3), part)
        slots = jnp.where(lane < half, pltpu.roll(slots, half, 1), slots)
        for k in range(2):
            store_planes(base + 3 + k, slots, slots, part)
            slots = pltpu.roll(slots, width - SLOT, 1)

    full_lane = lax.broadcasted_iota(jnp.int32, (depth, width), 1) < half

    def outer_plane(rp, k, step, dc):
        if k == 0:
            return pairs[base + rp + step, 1 + dc]
        slots = pairs[base + 3 + step, 1 + dc]
        if rp == 0:
            return jnp.where(full_lane, pairs[base + 1 + step, 1 + dc], slots)
        return jnp.where(full_lane, slots, pairs[base + step, 1 + dc])

    def outer_plan(rp, k):
        if k == 0:
            return (rp, rp), (2 * rows + 2 + rp, 4 + rp)
        return ((2, 1), "halo") if rp == 0 else ("halo", (2 * rows + 1, 4))

    own.wait()
    inner_pairs(mine)
    raw_copies[0].wait()
    turn(0, one_w)
    raw_copies[1].wait()
    side.wait()
    inner_pairs(theirs)
    for item in up_copies:
        item.wait()

    extras = upsample(inner_plane, h, inner_plan, False)
    slims = slim_near_far(extras[1], extras[0], SLOT)
    slims.append(slim_edges([(r, r - 3) for r in range(3, 2 * rows + 1)]))
    for n in range(3):
        slim[n] = slims[n]
    turn(1, two_w)
    conv_one(
        (range(3, 7), (None, 7, 8, 9), range(10, 2 * rows - 1)), slims, lambda r: r - 2
    )
    forward(0)
    forward(1)
    outer_pairs(mine)
    conv_two(range(3, 7))
    conv_two(range(7, 11))
    conv_two(range(11, 2 * rows - 3))
    arrived(0)
    arrived(1)
    outer_pairs(theirs)
    extras = upsample(outer_plane, 2, outer_plan, True)
    slims = slim_near_far(extras[0], extras[1], width - SLOT)
    slims.append(slim_edges([
        *((r, r) for r in range(5)), *((2 * rows - 1 + r, 5 + r) for r in range(5))
    ]))
    spot = cell // SLOT
    gone = ((spot < 2) & (ha == 0)) | ((spot >= 8) & (ha == ha_count - 1))
    for n in range(2):
        value = jnp.where(gone, blank, slims[n])
        value = jnp.where(spot == 3, pltpu.roll(slim[n], 3 * SLOT, 1), value)
        value = jnp.where(spot == 4, pltpu.roll(slim[n], 3 * SLOT, 1), value)
        old = pltpu.roll(slim[n], width - (2 * rows - 9) * SLOT, 1)
        slims[n] = jnp.where((spot == 5) | (spot == 6), old, value)
    conv_one(
        ((0, 1, 2, 2 * rows - 1), (None, 2 * rows, 2 * rows + 1)), slims,
        lambda r: r + 1 if r < 3 else r - (2 * rows - 7)
    )


def finish_kernel(ready, weight, skip, field3, dst, tail, sem):
    count, chans, width = skip.shape
    inner = pl.ds(3, count - 6)
    items = [pltpu.make_async_copy(ready.at[0, inner], dst.at[0, inner], sem.at[0])]
    items[0].start()
    spans = ((0, 1, 2), (count - 3, count - 2, count - 1))
    for n, span in enumerate(spans):
        spot = pl.ds(span[0], 3)
        items.append(pltpu.make_async_copy(tail.at[n], dst.at[0, spot], sem.at[1 + n]))
    begun = 0
    for group in ((0, 1, 2, count - 3), (count - 2, count - 1)):
        rhs = jnp.concatenate(
            [field3[pl.ds(r, 3)].reshape(9 * chans, width) for r in group], axis=1
        )
        total = jnp.dot(weight[...], rhs, preferred_element_type=f32)
        for k, r in enumerate(group):
            value = total[:, k * width:(k + 1) * width] + skip[r].astype(f32)
            n = 0 if r < 3 else 1
            tail[n, r - spans[n][0]] = value.astype(bf16)
        begun += 1
        items[begun].start()
    for item in items:
        item.wait()


def local(ha_count, latent, up_weight, conv_one, gain_one, conv_two, gain_two):
    _, rows, width, share = latent.shape
    chans = conv_one.shape[3]
    latent = jnp.transpose(latent, (0, 1, 3, 2))
    up_weight = jnp.transpose(up_weight, (0, 1, 3, 2))
    anywhere = pl.BlockSpec(memory_space=pl.ANY)
    vmem = pl.BlockSpec(memory_space=pltpu.VMEM)
    depth = 2 * share
    result = pl.pallas_call(
        functools.partial(block_kernel, ha_count),
        out_shape=[
            pltpu.VMEM((1, 2 * rows, chans, width), bf16),
            pltpu.VMEM((chans, 9 * chans), bf16),
            pltpu.VMEM((2 * rows, chans, width), bf16),
            pltpu.VMEM((2 * rows + 2, 3 * chans, width), bf16),
        ],
        in_specs=[anywhere] + [vmem] * 2 + [anywhere] * 3,
        out_specs=[vmem] * 4,
        scratch_shapes=[
            pltpu.VMEM((2, 2, chans, 4 * depth), bf16),
            pltpu.VMEM((2, 3, 3, chans, chans), bf16),
            pltpu.VMEM((chans, 9 * chans), bf16),
            pltpu.VMEM((rows + 4, depth, width), bf16),
            pltpu.VMEM((rows // 2 + 7, 3, depth, width), bf16),
            pltpu.VMEM((2 * rows + 4, 3 * chans, width), bf16),
            pltpu.VMEM((2, chans, width), f32),
            pltpu.VMEM((2 * width, 2 * width), bf16),
            pltpu.VMEM((3, chans, width), bf16),
            pltpu.SemaphoreType.DMA((4,)),
            pltpu.SemaphoreType.DMA((9,)),
            pltpu.SemaphoreType.DMA((9,)),
        ],
        compiler_params=pltpu.CompilerParams(
            vmem_limit_bytes=56000000, collective_id=0, has_side_effects=True
        ),
    )(latent, gain_one.reshape(1, chans), gain_two.reshape(1, chans),
      up_weight, conv_one, conv_two)
    result = pl.pallas_call(
        finish_kernel,
        out_shape=jax.ShapeDtypeStruct(result[0].shape, bf16),
        in_specs=[vmem] * 4,
        out_specs=pl.BlockSpec(memory_space=pltpu.HBM),
        scratch_shapes=[
            pltpu.VMEM((2, 3, chans, width), bf16),
            pltpu.SemaphoreType.DMA((3,)),
        ],
        compiler_params=pltpu.CompilerParams(vmem_limit_bytes=8 * 1024 * 1024),
    )(*result)
    return jnp.transpose(result, (0, 1, 3, 2))


def solution(mesh):
    return jax.shard_map(
        functools.partial(local, mesh.shape["ha"]),
        mesh=mesh,
        in_specs=(P("grp", "ha", None, "col"), P(), P(), P(), P(), P()),
        out_specs=P("grp", "ha", "col", None),
        check_vma=False,
    )
```

```python
import functools

import jax
import jax.numpy as jnp
from jax import lax
from jax.experimental import pallas as pl
from jax.experimental.pallas import tpu as pltpu
from jax.sharding import PartitionSpec as P

f32 = jnp.float32
bf16 = jnp.bfloat16
MESH = pl.DeviceIdType.MESH
SLOT = 8
SLOT_AT = 3
phase_taps = (((0, 1), (-1, 3)), ((0, 2), (1, 0)))


def activate(wide, half_gain):
    stats = jnp.sum(wide * wide, axis=0, keepdims=True) * (1.0 / wide.shape[0])
    half = wide * lax.rsqrt(stats + 1e-06) * half_gain
    return half * jnp.tanh(half) + half


def block_kernel(
    ha_count, lat, gain_one, gain_two, up_hbm, one_hbm, two_hbm, out, two_w, ups, second,
    up_w, raw, one_w, field, pairs, first, gains, perm,
    slim, sem, send, recv
):
    ha = lax.axis_index("ha")
    col = lax.axis_index("col")
    rows, share, width = lat.shape[1], lat.shape[2], lat.shape[3]
    chans = out.shape[2]
    half = width // 2
    depth = 2 * share
    mine = pl.ds(pl.multiple_of(col * share, share), share)
    other = {"col": 1 - col}
    has_above, has_below = ha > 0, ha < ha_count - 1

    barrier = pltpu.get_barrier_semaphore()
    pl.semaphore_signal(barrier, 1, device_id=other, device_id_type=MESH)

    @pl.when(has_above)
    def _():
        pl.semaphore_signal(barrier, 1, device_id={"ha": ha - 1}, device_id_type=MESH)

    @pl.when(has_below)
    def _():
        pl.semaphore_signal(barrier, 1, device_id={"ha": ha + 1}, device_id_type=MESH)

    own = pltpu.make_async_copy(lat.at[0], field.at[pl.ds(2, rows), mine], sem.at[0])
    own.start()
    raw_copies = [
        pltpu.make_async_copy(src, raw.at[n], sem.at[1 + n])
        for n, src in enumerate((one_hbm, two_hbm))
    ]
    for item in raw_copies:
        item.start()
    up_copies = []
    for rp in range(2):
        for cp in range(2):
            tap = 0
            for _, ra in phase_taps[rp]:
                for _, cb in phase_taps[cp]:
                    up_copies.append(pltpu.make_async_copy(
                        up_hbm.at[ra, cb],
                        up_w.at[rp, cp, :, pl.ds(tap * depth, depth)],
                        sem.at[3],
                    ))
                    tap += 1
    for item in up_copies:
        item.start()

    peers = 1 + jnp.minimum(ha, 1) + jnp.minimum(ha_count - 1 - ha, 1)
    pl.semaphore_wait(barrier, peers)

    def remote(src, dst, target, n):
        return pltpu.make_async_remote_copy(
            src_ref=src, dst_ref=dst, send_sem=send.at[n], recv_sem=recv.at[n],
            device_id=target, device_id_type=MESH,
        )

    side = remote(lat.at[0], field.at[pl.ds(2, rows), mine], other, 0)
    downs, ups_sent, pass_tops, pass_bottoms = [], [], [], []
    for n in range(2):
        top, bottom = field.at[1 - n, mine], field.at[rows + 2 + n, mine]
        downs.append(remote(lat.at[0, rows - 1 - n], top, {"ha": ha + 1}, 1 + n))
        ups_sent.append(remote(lat.at[0, n], bottom, {"ha": ha - 1}, 3 + n))
        pass_tops.append(remote(top, top, other, 5 + n))
        pass_bottoms.append(remote(bottom, bottom, other, 7 + n))

    for n in range(2):
        @pl.when(has_below)
        def _():
            downs[n].start()

        @pl.when(has_above)
        def _():
            ups_sent[n].start()

    side.start()

    @pl.when(ha == 0)
    def _():
        field[pl.ds(0, 2)] = jnp.zeros((2, depth, width), bf16)

    @pl.when(ha == ha_count - 1)
    def _():
        field[pl.ds(rows + 2, 2)] = jnp.zeros((2, depth, width), bf16)

    for n, gain in enumerate((gain_one, gain_two)):
        gains[n] = jnp.broadcast_to(gain[...] * 0.5, (width, chans)).T
    at = lax.broadcasted_iota(jnp.int32, (2 * width, 2 * width), 0)
    to = lax.broadcasted_iota(jnp.int32, (2 * width, 2 * width), 1)
    source = (to % 2) * width + (to // width) * half + (to % width) // 2
    perm[...] = (source == at).astype(f32).astype(bf16)

    def turn(n, turned):
        at = lax.broadcasted_iota(jnp.int32, (chans, chans), 0)
        to = lax.broadcasted_iota(jnp.int32, (chans, chans), 1)
        eye = (at == to).astype(f32).astype(bf16)
        taps = [raw[n, a, b] for a in range(3) for b in (2 - 2 * col, 1, 2 * col)]
        turned[...] = lax.dot_general(
            eye, jnp.concatenate(taps, axis=0), (((1,), (1,)), ((), ())),
            preferred_element_type=f32,
        ).astype(bf16)

    lane = lax.broadcasted_iota(jnp.int32, (share, width), 1)
    keep_near = (lane < half) == (col == 0)
    low = lane % half == 0
    high = lane % half == half - 1
    low_col = low & (col == 0)
    high_col = high & (col > 0)
    zero = jnp.zeros((share, width), bf16)

    def store_planes(n, here, there, part):
        pairs[n, 1, part] = here
        pairs[n, 0, part] = pltpu.roll(
            jnp.where(high_col, there, jnp.where(high, zero, here)), 1, 1
        )
        pairs[n, 2, part] = pltpu.roll(
            jnp.where(low_col, there, jnp.where(low, zero, here)), width - 1, 1
        )

    def halves(f, apart, part):
        near = field[f + apart * col, part]
        far = pltpu.roll(field[f + apart * (1 - col), part], half, 1)
        return jnp.where(keep_near, near, far), jnp.where(keep_near, far, near)

    def make_pair(n, f, apart, part):
        here, there = halves(f, apart, part)
        store_planes(n, here, there, part)

    def halo_slots(listed, part):
        total = zero
        for s, f in enumerate(listed):
            moved = pltpu.roll(field[f, part], SLOT * s + SLOT_AT + col, 1)
            total = jnp.where(lane // SLOT == half // SLOT + s, moved, total)
        return total

    cell = lax.broadcasted_iota(jnp.int32, (chans, width), 1)
    blank = jnp.zeros((chans, width), bf16)
    inward = 1 + (1 - col) * (width - 2)
    outward = 1 + col * (width - 2)
    joint_cell = cell == (1 - col) * (width - 1)
    rim_cell = cell == col * (width - 1)

    def place(field3, r, value, moved):
        turned_in = pltpu.roll(value, inward, 1)
        if moved is not None:
            turned_in = jnp.where(joint_cell, moved, turned_in)
        field3[r, pl.ds(chans, chans)] = value
        field3[r, pl.ds(0, chans)] = turned_in
        field3[r, pl.ds(2 * chans, chans)] = jnp.where(
            rim_cell, blank, pltpu.roll(value, outward, 1)
        )

    def framed(r, value):
        if r < 2:
            return jnp.where(has_above, value, jnp.zeros_like(value))
        if r >= 2 * rows + 2:
            return jnp.where(has_below, value, jnp.zeros_like(value))
        return value

    def upsample(plane, count, plan):
        extras = []
        parts = {}

        def phase(rp, cp):
            pieces = [
                jnp.concatenate([plane(rp, k, dr + 1 - rp, dc) for k in range(count)], axis=1)
                for dr, _ in phase_taps[rp] for dc, _ in phase_taps[cp]
            ]
            parts[rp, cp] = jnp.dot(
                up_w[rp, cp], jnp.concatenate(pieces, axis=0), preferred_element_type=f32
            ).astype(bf16)

        for cp in range(2):
            for rp in range(2):
                phase(rp, cp)
        for rp in range(2):
            extra = None
            for k in (count - 1, *range(count - 1)):
                cut = slice(k * width, (k + 1) * width)
                both = jnp.concatenate([parts[rp, 0][:, cut], parts[rp, 1][:, cut]], axis=1)
                mixed = jnp.dot(both, perm[...], preferred_element_type=f32)
                todo = plan(rp, k)
                for side_half in sorted(range(2), key=lambda x: todo[x] != "halo"):
                    value = mixed[:, side_half * width:(side_half + 1) * width]
                    act = activate(value, gains[0]).astype(bf16)
                    if todo[side_half] == "halo":
                        extra = act
                        continue
                    r, slot = todo[side_half]
                    if 2 <= r < 2 * rows + 2:
                        ups[r - 2] = value.astype(bf16)
                    moved = pltpu.roll(extra, width - 1 - 2 * SLOT_AT - 2 * SLOT * slot, 1)
                    place(first, r, framed(r, act), framed(r, moved))
            extras.append(extra)
        return extras

    def windows(field3, span):
        return jnp.concatenate(
            [field3[pl.ds(r, 3)].reshape(9 * chans, width) for r in span], axis=1
        )

    def slim_near_far(first_half, second_half, apart):
        return [
            jnp.where(
                cell % (2 * SLOT) == SLOT - 1,
                pltpu.roll(first_half, shift, 1),
                pltpu.roll(second_half, apart + shift, 1),
            )
            for shift in (col, 1 - col)
        ]

    def slim_edges(listed):
        total = blank
        for r, s in listed:
            moved = pltpu.roll(first[r, pl.ds(chans, chans)], SLOT * s + SLOT - col, 1)
            total = jnp.where(cell // SLOT == s, moved, total)
        return total

    def slim_windows(slims):
        return jnp.concatenate(
            [pltpu.roll(x, (SLOT * (1 - d)) % width, 1) if d != 1 else x
             for d in range(3) for x in slims], axis=0
        )

    def normed(total):
        return activate(total.astype(bf16).astype(f32), gains[1])

    def conv_one(span, slims, slot_of):
        totals = {}
        for group in span:
            rhs = jnp.concatenate([
                slim_windows(slims) if r is None else
                first[pl.ds(r, 3)].reshape(9 * chans, width) for r in group
            ], axis=1)
            total = jnp.dot(one_w[...], rhs, preferred_element_type=f32)
            for k, r in enumerate(group):
                totals[r] = total[:, k * width:(k + 1) * width]
        joint = normed(totals[None]).astype(bf16)
        for group in span:
            for r in group:
                if r is None:
                    continue
                act = normed(totals[r]).astype(bf16)
                moved = pltpu.roll(joint, width - SLOT * (slot_of(r) + 1) + col, 1)
                if r == 0 or r == 2 * rows + 1:
                    inside = has_above if r == 0 else has_below
                    act = jnp.where(inside, act, blank)
                    moved = jnp.where(inside, moved, blank)
                place(second, r, act, moved)

    def conv_two(span):
        total = jnp.dot(two_w[...], windows(second, span), preferred_element_type=f32)
        for k, r in enumerate(span):
            value = total[:, k * width:(k + 1) * width] + ups[r].astype(f32)
            out[0, r] = value.astype(bf16)

    def forward(n):
        @pl.when(has_above)
        def _():
            downs[n].wait_recv()
            pass_tops[n].start()

        @pl.when(has_below)
        def _():
            ups_sent[n].wait_recv()
            pass_bottoms[n].start()

    def arrived(n):
        @pl.when(has_above)
        def _():
            ups_sent[n].wait_send()
            pass_tops[n].wait()

        @pl.when(has_below)
        def _():
            downs[n].wait_send()
            pass_bottoms[n].wait()

    h = rows // 2
    theirs = pl.ds(pl.multiple_of((1 - col) * share, share), share)
    base = h + 2

    def inner_pairs(part):
        for k in range(h):
            make_pair(k, 2 + k, h, part)
        slots = halo_slots(range(2, rows + 2), part)
        for k in range(2):
            here, there = halves(1 + h + k, 0, part)
            here = jnp.where(lane < half, here, slots)
            store_planes(h + k, here, there, part)
            slots = pltpu.roll(slots, width - SLOT, 1)

    def inner_plane(rp, k, step, dc):
        return pairs[k + step if k < h - 1 else h + step, 1 + dc]

    def inner_plan(rp, k):
        r = 4 - rp + 2 * k
        if k == h - 1:
            return (r, k), "halo"
        return (r, k), (r + 2 * h, k + h)

    def outer_pairs(part):
        for k in range(3):
            make_pair(base + k, k, rows + 1, part)
        slots = halo_slots((0, 1, 2, 2, rows + 1, rows + 2, rows + 3), part)
        slots = jnp.where(lane < half, pltpu.roll(slots, half, 1), slots)
        for k in range(2):
            store_planes(base + 3 + k, slots, slots, part)
            slots = pltpu.roll(slots, width - SLOT, 1)

    full_lane = lax.broadcasted_iota(jnp.int32, (depth, width), 1) < half

    def outer_plane(rp, k, step, dc):
        if k == 0:
            return pairs[base + rp + step, 1 + dc]
        slots = pairs[base + 3 + step, 1 + dc]
        if rp == 0:
            return jnp.where(full_lane, pairs[base + 1 + step, 1 + dc], slots)
        return jnp.where(full_lane, slots, pairs[base + step, 1 + dc])

    def outer_plan(rp, k):
        if k == 0:
            return (rp, rp), (2 * rows + 2 + rp, 4 + rp)
        return ((2, 1), "halo") if rp == 0 else ("halo", (2 * rows + 1, 4))

    own.wait()
    inner_pairs(mine)
    for item in raw_copies:
        item.wait()
    turn(0, one_w)
    for item in up_copies:
        item.wait()
    side.wait()
    inner_pairs(theirs)
    extras = upsample(inner_plane, h, inner_plan)
    slims = slim_near_far(extras[1], extras[0], SLOT)
    slims.append(slim_edges([(r, r - 3) for r in range(3, 2 * rows + 1)]))
    for n in range(3):
        slim[n] = slims[n]
    turn(1, two_w)
    conv_one(
        (range(3, 7), (None, 7, 8, 9), range(10, 2 * rows - 1)), slims, lambda r: r - 2
    )
    forward(0)
    forward(1)
    outer_pairs(mine)
    conv_two(range(3, 7))
    conv_two(range(7, 11))
    arrived(0)
    arrived(1)
    conv_two(range(11, 2 * rows - 3))
    outer_pairs(theirs)
    extras = upsample(outer_plane, 2, outer_plan)
    slims = slim_near_far(extras[0], extras[1], width - SLOT)
    slims.append(slim_edges([
        *((r, r) for r in range(5)), *((2 * rows - 1 + r, 5 + r) for r in range(5))
    ]))
    spot = cell // SLOT
    gone = ((spot < 2) & (ha == 0)) | ((spot >= 8) & (ha == ha_count - 1))
    for n in range(2):
        value = jnp.where(gone, blank, slims[n])
        value = jnp.where(spot == 3, pltpu.roll(slim[n], 3 * SLOT, 1), value)
        value = jnp.where(spot == 4, pltpu.roll(slim[n], 3 * SLOT, 1), value)
        old = pltpu.roll(slim[n], width - (2 * rows - 9) * SLOT, 1)
        slims[n] = jnp.where((spot == 5) | (spot == 6), old, value)
    conv_one(
        ((0, 1, 2, 2 * rows - 1), (None, 2 * rows, 2 * rows + 1)), slims,
        lambda r: r + 1 if r < 3 else r - (2 * rows - 7)
    )


def finish_kernel(ready, weight, skip, field3, dst, tail, sem):
    count, chans, width = skip.shape
    inner = pl.ds(3, count - 6)
    items = [pltpu.make_async_copy(ready.at[0, inner], dst.at[0, inner], sem.at[0])]
    items[0].start()
    spans = ((0, 1, 2), (count - 3, count - 2, count - 1))
    for n, span in enumerate(spans):
        spot = pl.ds(span[0], 3)
        items.append(pltpu.make_async_copy(tail.at[n], dst.at[0, spot], sem.at[1 + n]))
    begun = 0
    for group in ((0, 1, 2, count - 3), (count - 2, count - 1)):
        rhs = jnp.concatenate(
            [field3[pl.ds(r, 3)].reshape(9 * chans, width) for r in group], axis=1
        )
        total = jnp.dot(weight[...], rhs, preferred_element_type=f32)
        for k, r in enumerate(group):
            value = total[:, k * width:(k + 1) * width] + skip[r].astype(f32)
            n = 0 if r < 3 else 1
            tail[n, r - spans[n][0]] = value.astype(bf16)
        begun += 1
        items[begun].start()
    for item in items:
        item.wait()


def local(ha_count, latent, up_weight, conv_one, gain_one, conv_two, gain_two):
    _, rows, width, share = latent.shape
    chans = conv_one.shape[3]
    latent = jnp.transpose(latent, (0, 1, 3, 2))
    up_weight = jnp.transpose(up_weight, (0, 1, 3, 2))
    anywhere = pl.BlockSpec(memory_space=pl.ANY)
    vmem = pl.BlockSpec(memory_space=pltpu.VMEM)
    depth = 2 * share
    result = pl.pallas_call(
        functools.partial(block_kernel, ha_count),
        out_shape=[
            pltpu.VMEM((1, 2 * rows, chans, width), bf16),
            pltpu.VMEM((chans, 9 * chans), bf16),
            pltpu.VMEM((2 * rows, chans, width), bf16),
            pltpu.VMEM((2 * rows + 2, 3 * chans, width), bf16),
        ],
        in_specs=[anywhere] + [vmem] * 2 + [anywhere] * 3,
        out_specs=[vmem] * 4,
        scratch_shapes=[
            pltpu.VMEM((2, 2, chans, 4 * depth), bf16),
            pltpu.VMEM((2, 3, 3, chans, chans), bf16),
            pltpu.VMEM((chans, 9 * chans), bf16),
            pltpu.VMEM((rows + 4, depth, width), bf16),
            pltpu.VMEM((rows // 2 + 7, 3, depth, width), bf16),
            pltpu.VMEM((2 * rows + 4, 3 * chans, width), bf16),
            pltpu.VMEM((2, chans, width), f32),
            pltpu.VMEM((2 * width, 2 * width), bf16),
            pltpu.VMEM((3, chans, width), bf16),
            pltpu.SemaphoreType.DMA((4,)),
            pltpu.SemaphoreType.DMA((9,)),
            pltpu.SemaphoreType.DMA((9,)),
        ],
        compiler_params=pltpu.CompilerParams(
            vmem_limit_bytes=56000000, collective_id=0, has_side_effects=True
        ),
    )(latent, gain_one.reshape(1, chans), gain_two.reshape(1, chans),
      up_weight, conv_one, conv_two)
    result = pl.pallas_call(
        finish_kernel,
        out_shape=jax.ShapeDtypeStruct(result[0].shape, bf16),
        in_specs=[vmem] * 4,
        out_specs=pl.BlockSpec(memory_space=pltpu.HBM),
        scratch_shapes=[
            pltpu.VMEM((2, 3, chans, width), bf16),
            pltpu.SemaphoreType.DMA((3,)),
        ],
        compiler_params=pltpu.CompilerParams(vmem_limit_bytes=8 * 1024 * 1024),
    )(*result)
    return jnp.transpose(result, (0, 1, 3, 2))


def solution(mesh):
    return jax.shard_map(
        functools.partial(local, mesh.shape["ha"]),
        mesh=mesh,
        in_specs=(P("grp", "ha", None, "col"), P(), P(), P(), P(), P()),
        out_specs=P("grp", "ha", "col", None),
        check_vma=False,
    )
```

```python
import functools

import jax
import jax.numpy as jnp
from jax import lax
from jax.experimental import pallas as pl
from jax.experimental.pallas import tpu as pltpu
from jax.sharding import PartitionSpec as P

f32 = jnp.float32
bf16 = jnp.bfloat16
MESH = pl.DeviceIdType.MESH
SLOT = 8
SLOT_AT = 3
phase_taps = (((0, 1), (-1, 3)), ((0, 2), (1, 0)))


def activate(wide, half_gain):
    stats = jnp.sum(wide * wide, axis=0, keepdims=True) * (1.0 / wide.shape[0])
    half = wide * lax.rsqrt(stats + 1e-06) * half_gain
    return half * jnp.tanh(half) + half


def block_kernel(
    ha_count, lat, gain_one, gain_two, up_hbm, one_hbm, two_hbm, out, two_w, ups, second,
    up_w, raw, one_w, field, pairs, first, gains, perm,
    slim, sem, send, recv
):
    ha = lax.axis_index("ha")
    col = lax.axis_index("col")
    rows, share, width = lat.shape[1], lat.shape[2], lat.shape[3]
    chans = out.shape[2]
    half = width // 2
    depth = 2 * share
    mine = pl.ds(pl.multiple_of(col * share, share), share)
    other = {"col": 1 - col}
    has_above, has_below = ha > 0, ha < ha_count - 1

    barrier = pltpu.get_barrier_semaphore()
    pl.semaphore_signal(barrier, 1, device_id=other, device_id_type=MESH)

    @pl.when(has_above)
    def _():
        pl.semaphore_signal(barrier, 1, device_id={"ha": ha - 1}, device_id_type=MESH)

    @pl.when(has_below)
    def _():
        pl.semaphore_signal(barrier, 1, device_id={"ha": ha + 1}, device_id_type=MESH)

    own = pltpu.make_async_copy(lat.at[0], field.at[pl.ds(2, rows), mine], sem.at[0])
    own.start()
    raw_copies = [
        pltpu.make_async_copy(src, raw.at[n], sem.at[1 + n])
        for n, src in enumerate((one_hbm, two_hbm))
    ]
    for item in raw_copies:
        item.start()
    up_copies = []
    for rp in range(2):
        for cp in range(2):
            tap = 0
            for _, ra in phase_taps[rp]:
                for _, cb in phase_taps[cp]:
                    up_copies.append(pltpu.make_async_copy(
                        up_hbm.at[ra, cb],
                        up_w.at[rp, cp, :, pl.ds(tap * depth, depth)],
                        sem.at[3],
                    ))
                    tap += 1
    for item in up_copies:
        item.start()

    peers = 1 + jnp.minimum(ha, 1) + jnp.minimum(ha_count - 1 - ha, 1)
    pl.semaphore_wait(barrier, peers)

    def remote(src, dst, target, n):
        return pltpu.make_async_remote_copy(
            src_ref=src, dst_ref=dst, send_sem=send.at[n], recv_sem=recv.at[n],
            device_id=target, device_id_type=MESH,
        )

    side = remote(lat.at[0], field.at[pl.ds(2, rows), mine], other, 0)
    downs, ups_sent, pass_tops, pass_bottoms = [], [], [], []
    for n in range(2):
        top, bottom = field.at[1 - n, mine], field.at[rows + 2 + n, mine]
        downs.append(remote(lat.at[0, rows - 1 - n], top, {"ha": ha + 1}, 1 + n))
        ups_sent.append(remote(lat.at[0, n], bottom, {"ha": ha - 1}, 3 + n))
        pass_tops.append(remote(top, top, other, 5 + n))
        pass_bottoms.append(remote(bottom, bottom, other, 7 + n))

    for n in range(2):
        @pl.when(has_below)
        def _():
            downs[n].start()

        @pl.when(has_above)
        def _():
            ups_sent[n].start()

    side.start()

    @pl.when(ha == 0)
    def _():
        field[pl.ds(0, 2)] = jnp.zeros((2, depth, width), bf16)

    @pl.when(ha == ha_count - 1)
    def _():
        field[pl.ds(rows + 2, 2)] = jnp.zeros((2, depth, width), bf16)

    for n, gain in enumerate((gain_one, gain_two)):
        gains[n] = jnp.broadcast_to(gain[...] * 0.5, (width, chans)).T
    at = lax.broadcasted_iota(jnp.int32, (2 * width, 2 * width), 0)
    to = lax.broadcasted_iota(jnp.int32, (2 * width, 2 * width), 1)
    source = (to % 2) * width + (to // width) * half + (to % width) // 2
    perm[...] = (source == at).astype(f32).astype(bf16)

    def turn(n, turned):
        at = lax.broadcasted_iota(jnp.int32, (chans, chans), 0)
        to = lax.broadcasted_iota(jnp.int32, (chans, chans), 1)
        eye = (at == to).astype(f32).astype(bf16)
        taps = [raw[n, a, b] for a in range(3) for b in (2 - 2 * col, 1, 2 * col)]
        turned[...] = lax.dot_general(
            eye, jnp.concatenate(taps, axis=0), (((1,), (1,)), ((), ())),
            preferred_element_type=f32,
        ).astype(bf16)

    lane = lax.broadcasted_iota(jnp.int32, (share, width), 1)
    keep_near = (lane < half) == (col == 0)
    low = lane % half == 0
    high = lane % half == half - 1
    low_col = low & (col == 0)
    high_col = high & (col > 0)
    zero = jnp.zeros((share, width), bf16)

    def store_planes(n, here, there, part):
        pairs[n, 1, part] = here
        pairs[n, 0, part] = pltpu.roll(
            jnp.where(high_col, there, jnp.where(high, zero, here)), 1, 1
        )
        pairs[n, 2, part] = pltpu.roll(
            jnp.where(low_col, there, jnp.where(low, zero, here)), width - 1, 1
        )

    def halves(f, apart, part):
        near = field[f + apart * col, part]
        far = pltpu.roll(field[f + apart * (1 - col), part], half, 1)
        return jnp.where(keep_near, near, far), jnp.where(keep_near, far, near)

    def make_pair(n, f, apart, part):
        here, there = halves(f, apart, part)
        store_planes(n, here, there, part)

    def halo_slots(listed, part):
        total = zero
        for s, f in enumerate(listed):
            moved = pltpu.roll(field[f, part], SLOT * s + SLOT_AT + col, 1)
            total = jnp.where(lane // SLOT == half // SLOT + s, moved, total)
        return total

    cell = lax.broadcasted_iota(jnp.int32, (chans, width), 1)
    blank = jnp.zeros((chans, width), bf16)
    inward = 1 + (1 - col) * (width - 2)
    outward = 1 + col * (width - 2)
    joint_cell = cell == (1 - col) * (width - 1)
    rim_cell = cell == col * (width - 1)

    def place(field3, r, value, moved):
        turned_in = pltpu.roll(value, inward, 1)
        if moved is not None:
            turned_in = jnp.where(joint_cell, moved, turned_in)
        field3[r, pl.ds(chans, chans)] = value
        field3[r, pl.ds(0, chans)] = turned_in
        field3[r, pl.ds(2 * chans, chans)] = jnp.where(
            rim_cell, blank, pltpu.roll(value, outward, 1)
        )

    def framed(r, value):
        if r < 2:
            return jnp.where(has_above, value, jnp.zeros_like(value))
        if r >= 2 * rows + 2:
            return jnp.where(has_below, value, jnp.zeros_like(value))
        return value

    def upsample(plane, count, plan):
        extras = []
        parts = {}

        def phase(rp, cp):
            pieces = [
                jnp.concatenate([plane(rp, k, dr + 1 - rp, dc) for k in range(count)], axis=1)
                for dr, _ in phase_taps[rp] for dc, _ in phase_taps[cp]
            ]
            parts[rp, cp] = jnp.dot(
                up_w[rp, cp], jnp.concatenate(pieces, axis=0), preferred_element_type=f32
            ).astype(bf16)

        for cp in range(2):
            for rp in range(2):
                phase(rp, cp)
        for rp in range(2):
            extra = None
            for k in (count - 1, *range(count - 1)):
                cut = slice(k * width, (k + 1) * width)
                both = jnp.concatenate([parts[rp, 0][:, cut], parts[rp, 1][:, cut]], axis=1)
                mixed = jnp.dot(both, perm[...], preferred_element_type=f32)
                todo = plan(rp, k)
                for side_half in sorted(range(2), key=lambda x: todo[x] != "halo"):
                    value = mixed[:, side_half * width:(side_half + 1) * width]
                    act = activate(value, gains[0]).astype(bf16)
                    if todo[side_half] == "halo":
                        extra = act
                        continue
                    r, slot = todo[side_half]
                    if 2 <= r < 2 * rows + 2:
                        ups[r - 2] = value.astype(bf16)
                    moved = pltpu.roll(extra, width - 1 - 2 * SLOT_AT - 2 * SLOT * slot, 1)
                    place(first, r, framed(r, act), framed(r, moved))
            extras.append(extra)
        return extras

    def windows(field3, span):
        return jnp.concatenate(
            [field3[pl.ds(r, 3)].reshape(9 * chans, width) for r in span], axis=1
        )

    def slim_near_far(first_half, second_half, apart):
        return [
            jnp.where(
                cell % (2 * SLOT) == SLOT - 1,
                pltpu.roll(first_half, shift, 1),
                pltpu.roll(second_half, apart + shift, 1),
            )
            for shift in (col, 1 - col)
        ]

    def slim_edges(listed):
        total = blank
        for r, s in listed:
            moved = pltpu.roll(first[r, pl.ds(chans, chans)], SLOT * s + SLOT - col, 1)
            total = jnp.where(cell // SLOT == s, moved, total)
        return total

    def slim_windows(slims):
        return jnp.concatenate(
            [pltpu.roll(x, (SLOT * (1 - d)) % width, 1) if d != 1 else x
             for d in range(3) for x in slims], axis=0
        )

    def normed(total):
        return activate(total.astype(bf16).astype(f32), gains[1])

    def conv_one(span, slims, slot_of):
        totals = {}
        for group in span:
            rhs = jnp.concatenate([
                slim_windows(slims) if r is None else
                first[pl.ds(r, 3)].reshape(9 * chans, width) for r in group
            ], axis=1)
            total = jnp.dot(one_w[...], rhs, preferred_element_type=f32)
            for k, r in enumerate(group):
                totals[r] = total[:, k * width:(k + 1) * width]
        joint = normed(totals[None]).astype(bf16)
        for group in span:
            for r in group:
                if r is None:
                    continue
                act = normed(totals[r]).astype(bf16)
                moved = pltpu.roll(joint, width - SLOT * (slot_of(r) + 1) + col, 1)
                if r == 0 or r == 2 * rows + 1:
                    inside = has_above if r == 0 else has_below
                    act = jnp.where(inside, act, blank)
                    moved = jnp.where(inside, moved, blank)
                place(second, r, act, moved)

    def conv_two(span):
        total = jnp.dot(two_w[...], windows(second, span), preferred_element_type=f32)
        for k, r in enumerate(span):
            value = total[:, k * width:(k + 1) * width] + ups[r].astype(f32)
            out[0, r] = value.astype(bf16)

    def forward(n):
        @pl.when(has_above)
        def _():
            downs[n].wait_recv()
            pass_tops[n].start()

        @pl.when(has_below)
        def _():
            ups_sent[n].wait_recv()
            pass_bottoms[n].start()

    def arrived(n):
        @pl.when(has_above)
        def _():
            ups_sent[n].wait_send()
            pass_tops[n].wait()

        @pl.when(has_below)
        def _():
            downs[n].wait_send()
            pass_bottoms[n].wait()

    h = rows // 2
    theirs = pl.ds(pl.multiple_of((1 - col) * share, share), share)
    base = h + 2

    def inner_pairs(part):
        for k in range(h):
            make_pair(k, 2 + k, h, part)
        slots = halo_slots(range(2, rows + 2), part)
        for k in range(2):
            here, there = halves(1 + h + k, 0, part)
            here = jnp.where(lane < half, here, slots)
            store_planes(h + k, here, there, part)
            slots = pltpu.roll(slots, width - SLOT, 1)

    def inner_plane(rp, k, step, dc):
        return pairs[k + step if k < h - 1 else h + step, 1 + dc]

    def inner_plan(rp, k):
        r = 4 - rp + 2 * k
        if k == h - 1:
            return (r, k), "halo"
        return (r, k), (r + 2 * h, k + h)

    def outer_pairs(part):
        for k in range(3):
            make_pair(base + k, k, rows + 1, part)
        slots = halo_slots((0, 1, 2, 2, rows + 1, rows + 2, rows + 3), part)
        slots = jnp.where(lane < half, pltpu.roll(slots, half, 1), slots)
        for k in range(2):
            store_planes(base + 3 + k, slots, slots, part)
            slots = pltpu.roll(slots, width - SLOT, 1)

    full_lane = lax.broadcasted_iota(jnp.int32, (depth, width), 1) < half

    def outer_plane(rp, k, step, dc):
        if k == 0:
            return pairs[base + rp + step, 1 + dc]
        slots = pairs[base + 3 + step, 1 + dc]
        if rp == 0:
            return jnp.where(full_lane, pairs[base + 1 + step, 1 + dc], slots)
        return jnp.where(full_lane, slots, pairs[base + step, 1 + dc])

    def outer_plan(rp, k):
        if k == 0:
            return (rp, rp), (2 * rows + 2 + rp, 4 + rp)
        return ((2, 1), "halo") if rp == 0 else ("halo", (2 * rows + 1, 4))

    own.wait()
    inner_pairs(mine)
    for item in raw_copies:
        item.wait()
    turn(0, one_w)
    for item in up_copies:
        item.wait()
    side.wait()
    inner_pairs(theirs)
    extras = upsample(inner_plane, h, inner_plan)
    slims = slim_near_far(extras[1], extras[0], SLOT)
    slims.append(slim_edges([(r, r - 3) for r in range(3, 2 * rows + 1)]))
    for n in range(3):
        slim[n] = slims[n]
    turn(1, two_w)
    conv_one(
        (range(3, 7), (None, 7, 8, 9), range(10, 2 * rows - 1)), slims, lambda r: r - 2
    )
    forward(0)
    forward(1)
    outer_pairs(mine)
    conv_two(range(3, 7))
    arrived(0)
    arrived(1)
    conv_two(range(7, 11))
    conv_two(range(11, 2 * rows - 3))
    outer_pairs(theirs)
    extras = upsample(outer_plane, 2, outer_plan)
    slims = slim_near_far(extras[0], extras[1], width - SLOT)
    slims.append(slim_edges([
        *((r, r) for r in range(5)), *((2 * rows - 1 + r, 5 + r) for r in range(5))
    ]))
    spot = cell // SLOT
    gone = ((spot < 2) & (ha == 0)) | ((spot >= 8) & (ha == ha_count - 1))
    for n in range(2):
        value = jnp.where(gone, blank, slims[n])
        value = jnp.where(spot == 3, pltpu.roll(slim[n], 3 * SLOT, 1), value)
        value = jnp.where(spot == 4, pltpu.roll(slim[n], 3 * SLOT, 1), value)
        old = pltpu.roll(slim[n], width - (2 * rows - 9) * SLOT, 1)
        slims[n] = jnp.where((spot == 5) | (spot == 6), old, value)
    conv_one(
        ((0, 1, 2, 2 * rows - 1, 2 * rows, 2 * rows + 1, None),), slims,
        lambda r: r + 1 if r < 3 else r - (2 * rows - 7)
    )


def finish_kernel(ready, weight, skip, field3, dst, tail, sem):
    count, chans, width = skip.shape
    inner = pl.ds(3, count - 6)
    items = [pltpu.make_async_copy(ready.at[0, inner], dst.at[0, inner], sem.at[0])]
    items[0].start()
    spans = ((0, 1, 2), (count - 3, count - 2, count - 1))
    for n, span in enumerate(spans):
        spot = pl.ds(span[0], 3)
        items.append(pltpu.make_async_copy(tail.at[n], dst.at[0, spot], sem.at[1 + n]))
    begun = 0
    for group in ((0, 1, 2, count - 3), (count - 2, count - 1)):
        rhs = jnp.concatenate(
            [field3[pl.ds(r, 3)].reshape(9 * chans, width) for r in group], axis=1
        )
        total = jnp.dot(weight[...], rhs, preferred_element_type=f32)
        for k, r in enumerate(group):
            value = total[:, k * width:(k + 1) * width] + skip[r].astype(f32)
            n = 0 if r < 3 else 1
            tail[n, r - spans[n][0]] = value.astype(bf16)
        begun += 1
        items[begun].start()
    for item in items:
        item.wait()


def local(ha_count, latent, up_weight, conv_one, gain_one, conv_two, gain_two):
    _, rows, width, share = latent.shape
    chans = conv_one.shape[3]
    latent = jnp.transpose(latent, (0, 1, 3, 2))
    up_weight = jnp.transpose(up_weight, (0, 1, 3, 2))
    anywhere = pl.BlockSpec(memory_space=pl.ANY)
    vmem = pl.BlockSpec(memory_space=pltpu.VMEM)
    depth = 2 * share
    result = pl.pallas_call(
        functools.partial(block_kernel, ha_count),
        out_shape=[
            pltpu.VMEM((1, 2 * rows, chans, width), bf16),
            pltpu.VMEM((chans, 9 * chans), bf16),
            pltpu.VMEM((2 * rows, chans, width), bf16),
            pltpu.VMEM((2 * rows + 2, 3 * chans, width), bf16),
        ],
        in_specs=[anywhere] + [vmem] * 2 + [anywhere] * 3,
        out_specs=[vmem] * 4,
        scratch_shapes=[
            pltpu.VMEM((2, 2, chans, 4 * depth), bf16),
            pltpu.VMEM((2, 3, 3, chans, chans), bf16),
            pltpu.VMEM((chans, 9 * chans), bf16),
            pltpu.VMEM((rows + 4, depth, width), bf16),
            pltpu.VMEM((rows // 2 + 7, 3, depth, width), bf16),
            pltpu.VMEM((2 * rows + 4, 3 * chans, width), bf16),
            pltpu.VMEM((2, chans, width), f32),
            pltpu.VMEM((2 * width, 2 * width), bf16),
            pltpu.VMEM((3, chans, width), bf16),
            pltpu.SemaphoreType.DMA((4,)),
            pltpu.SemaphoreType.DMA((9,)),
            pltpu.SemaphoreType.DMA((9,)),
        ],
        compiler_params=pltpu.CompilerParams(
            vmem_limit_bytes=56000000, collective_id=0, has_side_effects=True
        ),
    )(latent, gain_one.reshape(1, chans), gain_two.reshape(1, chans),
      up_weight, conv_one, conv_two)
    result = pl.pallas_call(
        finish_kernel,
        out_shape=jax.ShapeDtypeStruct(result[0].shape, bf16),
        in_specs=[vmem] * 4,
        out_specs=pl.BlockSpec(memory_space=pltpu.HBM),
        scratch_shapes=[
            pltpu.VMEM((2, 3, chans, width), bf16),
            pltpu.SemaphoreType.DMA((3,)),
        ],
        compiler_params=pltpu.CompilerParams(vmem_limit_bytes=8 * 1024 * 1024),
    )(*result)
    return jnp.transpose(result, (0, 1, 3, 2))


def solution(mesh):
    return jax.shard_map(
        functools.partial(local, mesh.shape["ha"]),
        mesh=mesh,
        in_specs=(P("grp", "ha", None, "col"), P(), P(), P(), P(), P()),
        out_specs=P("grp", "ha", "col", None),
        check_vma=False,
    )
```
